256 devices in a mesh: leaf: 256 (over y, z, x, core).
Axes of the slice: x: 4, y: 4, z: 8, core: 2. Of those that a mesh axis runs over, the one named last changes fastest.
Arguments:
- white_noise: float32 [262144, 128], P('leaf'), may hold values from -6 to 6
- leaf_inverse: float32 [262144, 1024], P('leaf'), may hold values from -1 to 4, as said below
- bases: float32 [262144, 1024], P('leaf'), may hold values from -2 to 2
Outputs:
- solution: float32 [262144, 128], P('leaf')
The draws below stay inside these ranges and needn't reach their ends.
Inputs may be any that keep to these rules, and one draw needn't show every extreme that they name: `leaf_inverse`: each leaf's block of 1024 rows is symmetric positive definite.
All inputs are finite; a program needn't handle non-finite values.
Results may differ from the reference program's by a relative error of at most 0.0001.
Values sent between devices are 32-bit elements; how exact they have to be, the bound alone decides.
No kernel may reach another device: no remote copies, remote signals or barrier semaphores. Data moves between devices by JAX's collectives and lax.ppermute only.
A program may use at most 128 MiB of HBM per device.

```python
import math
import jax
import jax.numpy as jnp
from jax import lax

LEAF = 1024
R = 128
SAMPLES = 128
LEVELS = 8
NCELLS = 262144
N_LEAF = 256


def draw_leaf_inverse(key, part):
    key_diag = jax.random.fold_in(key, 11)
    key_sym = jax.random.fold_in(key, 12)
    raw = jnp.clip(jax.random.normal(key_sym, (N_LEAF, LEAF, LEAF), jnp.float32), -4.0, 4.0)
    diagonal = jax.random.uniform(key_diag, (N_LEAF, LEAF), jnp.float32, minval=1.0, maxval=2.0)
    symmetric = (raw + jnp.swapaxes(raw, 1, 2)) * (0.25 / math.sqrt(LEAF))
    matrix = symmetric + diagonal[:, :, None] * jnp.eye(LEAF, dtype=jnp.float32)[None, :, :]
    return matrix.reshape(N_LEAF * LEAF, LEAF)


def draw_bases(key, part):
    key_main = jax.random.fold_in(key, 21)
    scales = 2.0 / jnp.sqrt(LEAF * 2.0 ** (jnp.arange(LEVELS).astype(jnp.float32) + 1.0))
    raw = jnp.clip(jax.random.normal(key_main, (N_LEAF * LEAF, LEVELS, R), jnp.float32), -4.0, 4.0)
    return (raw * scales[None, :, None]).reshape(N_LEAF * LEAF, LEVELS * R)


def shard_levels(rng, extent, split, least, top_value):
    def one(dim, shards_of):
        steps = jax.random.uniform(jax.random.fold_in(jax.random.fold_in(rng, 6), dim), (shards_of,), jnp.float32, least / len(split), top_value / len(split))
        return jnp.repeat(jnp.exp(steps), extent[dim] // shards_of).reshape((-1,) + (1,) * (len(extent) - dim - 1))

    factor_of = one(*split[0])
    for cut in split[1:]:
        factor_of = factor_of * one(*cut)
    return factor_of


def scatter_about(stream_key, extent, deviation, limit, shards=(), held_as=jnp.bfloat16):
    level = shard_levels(stream_key, extent, shards, -0.22, 0.18) if shards else 1.0
    result = jax.random.normal(stream_key, extent, jnp.float32) * deviation * level
    return jnp.minimum(jnp.maximum(result, -limit), limit).astype(held_as)


def setup_inputs(seed: int = 0) -> dict:
    splits = jax.random.split(jax.random.key(seed), 4)
    white_noise = scatter_about(splits[0], (NCELLS, SAMPLES), 1.0, 6.0, ((0, 256),), jnp.float32)
    leaf_inverse = draw_leaf_inverse(jax.random.fold_in(splits[3], 71), 0)
    bases = draw_bases(jax.random.fold_in(splits[3], 71), 0)
    return dict(white_noise=white_noise, leaf_inverse=leaf_inverse, bases=bases)


def reference(white_noise, leaf_inverse, bases):
    matrices = leaf_inverse.reshape(N_LEAF, LEAF, LEAF)
    combined = jnp.concatenate([bases, white_noise], axis=1).reshape(N_LEAF, LEAF, LEVELS * R + SAMPLES)
    solved = jnp.einsum('nij,njc->nic', matrices, combined, precision=lax.Precision.HIGHEST)
    basis_all = bases.reshape(N_LEAF, LEAF, LEVELS * R)
    for tree_level in range(LEVELS):
        width_leaves = 2 ** (tree_level + 1)
        level_basis = basis_all[:, :, tree_level * R:(tree_level + 1) * R]
        products = jnp.einsum('nkr,nkc->nrc', level_basis, solved, precision=lax.Precision.HIGHEST)
        group_sums = products.reshape(N_LEAF // width_leaves, width_leaves, R, -1).sum(axis=1)
        capacity = jnp.eye(R, dtype=jnp.float32) + group_sums[:, :, :R]
        factor = jnp.linalg.cholesky(capacity)
        forward = jax.scipy.linalg.solve_triangular(factor, group_sums[:, :, R:], lower=True)
        weights = jax.scipy.linalg.solve_triangular(factor, forward, lower=True, trans=1)
        spread = jnp.repeat(weights, width_leaves, axis=0)
        solved = solved[:, :, R:] - jnp.einsum('nkr,nrc->nkc', solved[:, :, :R], spread, precision=lax.Precision.HIGHEST)
    return solved.reshape(N_LEAF * LEAF, SAMPLES)
```

```python
import jax
import jax.numpy as jnp
from jax import lax
from jax.experimental import pallas as pl
from jax.experimental.pallas import tpu as pltpu
from jax.sharding import PartitionSpec as P


R = 128
HALF = R // 2
QUARTER = HALF // 4
LEVELS = 8
F32 = jnp.float32
CORE_MASK = 1
RING_MASKS = (2, 4, 6)


def swap(value, mask):
    return lax.ppermute(value, "leaf", [(i, i ^ mask) for i in range(lax.axis_size("leaf"))])


def high_dot(a, b):
    return jnp.dot(a, b, precision=lax.Precision.HIGH, preferred_element_type=F32)


def split(v):
    high = v.astype(jnp.bfloat16)
    return high, (v - high.astype(F32)).astype(jnp.bfloat16)


def dot_split(a, b, contract=(1, 0)):
    dims = (((contract[0],), (contract[1],)), ((), ()))

    def one(p, q):
        return lax.dot_general(p, q, dims, preferred_element_type=F32)

    return one(a[0], b[0]) + (one(a[0], b[1]) + one(a[1], b[0]))


def cols(parts, start, stop):
    return tuple(part[:, start:stop] for part in parts)


def row_blocks(first):
    offset = 0
    out = []
    for m in range(first, LEVELS):
        width = (LEVELS + 1 - m) * R
        out.append((m, offset, width))
        offset += width
    return out, offset


def spd_inverse(rows):
    shape = (8, R)
    sub = lax.broadcasted_iota(jnp.int32, shape, 0)
    lane = lax.broadcasted_iota(jnp.int32, shape, 1)

    def spread_row(v, i):
        return jnp.broadcast_to(v[i : i + 1, :], shape)

    def spread_col(v, k):
        return jnp.broadcast_to(v[:, k : k + 1], shape)

    count = R // 8
    turns = 4
    per_turn = count // turns

    def eliminate(rows, p):
        rows = list(rows)
        panel = rows[p]
        base = 8 * p
        panel_rows = [spread_row(panel, j) for j in range(8)]
        d = [spread_col(panel, base + j) for j in range(8)]
        for a in range(0, 8, 2):
            b = a + 1
            ra = [spread_row(d[j], a) for j in range(8)]
            rb = [spread_row(d[j], b) for j in range(8)]
            inv_det = 1.0 / (ra[a] * rb[b] - ra[b] * rb[a])
            ma, mb = sub == a, sub == b
            ca, cb = d[a], d[b]
            ta = (ca * rb[b] - cb * rb[a]) * inv_det
            tb = (cb * ra[a] - ca * ra[b]) * inv_det
            iaa, iab = rb[b] * inv_det, -(ra[b] * inv_det)
            iba, ibb = -(rb[a] * inv_det), ra[a] * inv_det
            for j in range(8):
                if j == a:
                    d[j] = jnp.where(ma, iaa, jnp.where(mb, iba, -ta))
                elif j == b:
                    d[j] = jnp.where(ma, iab, jnp.where(mb, ibb, -tb))
                else:
                    na = iaa * ra[j] + iab * rb[j]
                    nb = iba * ra[j] + ibb * rb[j]
                    d[j] = jnp.where(ma, na, jnp.where(mb, nb, d[j] - (ta * ra[j] + tb * rb[j])))
        inside = (lane >= base) & (lane < base + 8)
        panel = None
        for j in range(8):
            term = d[j] * jnp.where(inside, jnp.where(lane == base + j, 1.0, 0.0), panel_rows[j])
            panel = term if panel is None else panel + term
        rows[p] = panel
        spread = [spread_row(panel, j) for j in range(8)]
        for step in range(1, count):
            i = (p + step) % count
            c = rows[i]
            total = None
            for j in range(0, 8, 2):
                pair = spread_col(c, base + j) * spread[j] + spread_col(c, base + j + 1) * spread[j + 1]
                total = pair if total is None else total + pair
            rows[i] = jnp.where(inside, 0.0, c) - total
        return rows

    def turn(_, rows):
        for p in range(per_turn):
            rows = eliminate(rows, p)
        rows = rows[per_turn:] + rows[:per_turn]
        return tuple(pltpu.roll(row, R - 8 * per_turn, 1) for row in rows)

    return list(lax.fori_loop(0, turns, turn, tuple(rows)))


def vmem(n):
    return [pl.BlockSpec(memory_space=pltpu.VMEM)] * n


def smem():
    return [pl.BlockSpec(memory_space=pltpu.SMEM)]


def out(*shape):
    return jax.ShapeDtypeStruct(shape, F32)


def call(kernel, outs, args, index=None, scratch=(), flops=0):
    moved = 4 * (sum(a.size for a in args) + sum(o.size for o in outs))
    head = [] if index is None else [index]
    return pl.pallas_call(
        kernel,
        out_shape=outs,
        in_specs=(smem() if head else []) + vmem(len(args)),
        out_specs=vmem(len(outs)),
        scratch_shapes=list(scratch),
        cost_estimate=pl.CostEstimate(flops=flops, bytes_accessed=moved, transcendentals=0),
        compiler_params=pltpu.CompilerParams(vmem_limit_bytes=16 << 20),
    )(*head, *args)


def first_rows_kernel(x_ref, u_ref, w_ref, row0_ref, row1_ref):
    x = split(x_ref[...])
    u = split(u_ref[...])
    w = split(w_ref[...])
    x0, x1 = cols(x, 0, R), cols(x, R, 2 * R)
    row0_ref[:, : LEVELS * R] = dot_split(x0, u, (0, 0))
    row0_ref[:, LEVELS * R :] = dot_split(x0, w, (0, 0))
    row1_ref[:, : (LEVELS - 1) * R] = dot_split(x1, cols(u, R, LEVELS * R), (0, 0))
    row1_ref[:, (LEVELS - 1) * R :] = dot_split(x1, w, (0, 0))


def second_rows_kernel(index_ref, a_ref, u_ref, w_ref, x_ref, keep_ref, send_ref):
    core = index_ref[0] & 1
    for r in range(4):
        rows = slice(r * 2 * R, (r + 1) * 2 * R)
        x_ref[rows, :] = dot_split(split(a_ref[rows, :]), split(u_ref[:, 2 * R : 3 * R]))
    x = split(x_ref[...])
    last = (LEVELS - 2) * R
    for span, operand in ((slice(0, last), u_ref[:, 2 * R :]), (slice(last, last + R), w_ref[...])):
        piece = dot_split(x, split(operand), (0, 0))
        keep_ref[:, span] = jnp.where(core == 0, piece[:HALF], piece[HALF:])
        send_ref[:, span] = jnp.where(core == 0, piece[HALF:], piece[:HALF])


def tail_solve_kernel(a_ref, u_ref, w_ref, x_ref, high_ref, low_ref):
    tail = (LEVELS - 3) * R
    high_ref[:, :tail], low_ref[:, :tail] = split(u_ref[:, 3 * R :])
    high_ref[:, tail:], low_ref[:, tail:] = split(w_ref[...])

    @pl.loop(0, 4)
    def _(r):
        rows = pl.ds(pl.multiple_of(r * 2 * R, 2 * R), 2 * R)
        x_ref[rows, :] = dot_split(split(a_ref[rows, :]), (high_ref[...], low_ref[...]))


def rest_rows_kernel(index_ref, u_ref, x_ref, keep_ref, send_ref):
    core = index_ref[0] & 1
    x = split(x_ref[...])
    for m, at, width in row_blocks(3)[0]:
        u = split(u_ref[:, m * R : (m + 1) * R])
        piece = dot_split(u, cols(x, (m - 3) * R, (LEVELS - 2) * R), (0, 0))
        keep_ref[:, at : at + width] = jnp.where(core == 0, piece[:HALF], piece[HALF:])
        send_ref[:, at : at + width] = jnp.where(core == 0, piece[HALF:], piece[:HALF])


def invert_store(panel_ref, w_ref):
    rows = [panel_ref[8 * i : 8 * i + 8, :R] for i in range(R // 8)]
    sub = lax.broadcasted_iota(jnp.int32, (8, R), 0)
    lane = lax.broadcasted_iota(jnp.int32, (8, R), 1)
    rows = [row + jnp.where(lane == sub + 8 * i, 1.0, 0.0) for i, row in enumerate(rows)]
    inverse = split(jnp.concatenate(spd_inverse(rows), axis=0))
    w_ref[...] = dot_split(inverse, split(panel_ref[:, R:]))


def invert_sum_kernel(own_ref, got_ref, panel_ref, w_ref):
    panel_ref[...] = own_ref[...] + got_ref[...]
    invert_store(panel_ref, w_ref)


def invert_half_kernel(index_ref, own_ref, got_ref, panel_ref, w_ref):
    core = index_ref[0] & 1
    own, got = own_ref[...], got_ref[...]
    panel_ref[:HALF, :] = jnp.where(core == 0, own, got)
    panel_ref[HALF:, :] = jnp.where(core == 0, got, own)
    invert_store(panel_ref, w_ref)


def invert_ring_kernel(index_ref, own_ref, got_ref, panel_ref, w_ref):
    core = index_ref[0] & 1
    x = (index_ref[0] >> 1) & 3
    for k in range(4):
        at = QUARTER * jnp.bitwise_xor(x, k)
        mine = pl.multiple_of(core * HALF + at, QUARTER)
        other = pl.multiple_of((1 - core) * HALF + at, QUARTER)
        panel_ref[pl.ds(mine, QUARTER), :] = own_ref[k]
        panel_ref[pl.ds(other, QUARTER), :] = got_ref[k]
    invert_store(panel_ref, w_ref)


def invert(level, own, got, index):
    n = (LEVELS + 1 - level) * R
    outs = (out(R, n), out(R, n - R))
    flops = 6 * R * R * n + 2 * R * R * R * 40
    if level == 0:
        return call(invert_sum_kernel, outs, (own, got), flops=flops)
    kernel = invert_ring_kernel if 3 <= level <= 5 else invert_half_kernel
    return call(kernel, outs, (own, got), index=index, flops=flops)


def row1_kernel(index_ref, own_ref, got_ref, keep_ref, got2_ref, panel_ref, w_ref, row_ref, half_ref, half2_ref):
    core = index_ref[0] & 1
    w = split(w_ref[...])
    row = own_ref[...] + got_ref[...] - dot_split(split(panel_ref[:, R : 2 * R]), w, (0, 0))
    row_ref[...] = row
    half_ref[...] = jnp.where(core == 0, row[:HALF], row[HALF:])
    change = dot_split(split(panel_ref[:, 2 * R : 3 * R]), cols(w, R, LEVELS * R), (0, 0))
    half2_ref[...] = keep_ref[...] + got2_ref[...] - jnp.where(core == 0, change[:HALF], change[HALF:])


def ahead_kernel(index_ref, own_ref, got_ref, panel_ref, w_ref, half_ref):
    core = index_ref[0] & 1
    change = dot_split(split(panel_ref[:, R : 2 * R]), split(w_ref[...]), (0, 0))
    half_ref[...] = own_ref[...] + got_ref[...] - jnp.where(core == 0, change[:HALF], change[HALF:])


def downdate(core, level, panel_ref, w_ref, rows):
    w = split(w_ref[...])
    for m, offset, width in rows:
        left = split(panel_ref[:, (m - level) * R : (m - level + 1) * R])
        full = dot_split(left, cols(w, (m - level - 1) * R, (LEVELS - level) * R), (0, 0))
        yield m, offset, width, jnp.where(core == 0, full[:HALF], full[HALF:])


def rest0_kernel(index_ref, own_ref, got_ref, panel_ref, w_ref, rest_ref):
    core = index_ref[0] & 1
    for m, at, width, change in downdate(core, 0, panel_ref, w_ref, row_blocks(3)[0]):
        span = slice(at, at + width)
        rest_ref[:, span] = own_ref[:, span] + got_ref[:, span] - change


def whole_downdate(level, panel_ref, w_ref, rows, scr):
    w = split(w_ref[...])
    for m, at, width in rows:
        left = split(panel_ref[:, (m - level) * R : (m - level + 1) * R])
        scr[:, at : at + width] = dot_split(left, cols(w, (m - level - 1) * R, (LEVELS - level) * R), (0, 0))


def quarter_at(index_ref, k):
    x = (index_ref[0] >> 1) & 3
    return QUARTER * jnp.bitwise_xor(x, k)


def update1_kernel(index_ref, rest_ref, panel_ref, w_ref, q0, q1, q2, q3, scr):
    core = index_ref[0] & 1
    whole_downdate(1, panel_ref, w_ref, row_blocks(3)[0], scr)
    for k, q in enumerate((q0, q1, q2, q3)):
        at = quarter_at(index_ref, k)
        mine = pl.multiple_of(at, QUARTER)
        both = pl.multiple_of(core * HALF + at, QUARTER)
        q[...] = rest_ref[pl.ds(mine, QUARTER), :] - scr[pl.ds(both, QUARTER), :]


def update_quarter_kernel(level):
    skip = (LEVELS + 1 - level) * R if level > 2 else 0

    def kernel(index_ref, rest_ref, panel_ref, w_ref, out_ref, scr):
        core = index_ref[0] & 1
        whole_downdate(level, panel_ref, w_ref, row_blocks(level + 1)[0], scr)
        at = pl.multiple_of(core * HALF + quarter_at(index_ref, 0), QUARTER)
        out_ref[...] = rest_ref[:, skip:] - scr[pl.ds(at, QUARTER), :]

    return kernel


def store_next(level, m, at, value, row_ref, rest_ref):
    if m == level + 1:
        row_ref[...] = value
    else:
        at -= (LEVELS - level) * R
        rest_ref[:, at : at + value.shape[1]] = value


def update5_kernel(index_ref, own_ref, panel_ref, w_ref, row_ref, rest_ref, scr):
    core = index_ref[0] & 1
    for k in range(4):
        at = pl.multiple_of(quarter_at(index_ref, k), QUARTER)
        scr[pl.ds(at, QUARTER), :] = own_ref[k]
    skip = (LEVELS + 1 - 5) * R
    for m, at, width, change in downdate(core, 5, panel_ref, w_ref, row_blocks(6)[0]):
        store_next(5, m, at, scr[:, skip + at : skip + at + width] - change, row_ref, rest_ref)


def update6_kernel(index_ref, own_ref, got_ref, panel_ref, w_ref, row_ref):
    core = index_ref[0] & 1
    for _, _, _, change in downdate(core, 6, panel_ref, w_ref, row_blocks(7)[0]):
        row_ref[...] = own_ref[...] + got_ref[...] - change


def last_kernel(solved_ref, w_ref, solution_ref):
    first = dot_split(split(solved_ref[:, :R]), split(w_ref[...]))
    solution_ref[...] = solved_ref[:, R:] - first


def update_flops(level):
    return sum(6 * R * R * width for _, _, width in row_blocks(level + 1)[0])


def ring_all(value):
    return jnp.stack([value] + [swap(value, mask) for mask in RING_MASKS])


def tree_solve(white_noise, leaf_inverse, bases):
    index = lax.axis_index("leaf").astype(jnp.int32).reshape(1)
    leaf = leaf_inverse.shape[0]
    x_head = high_dot(leaf_inverse, bases[:, : 2 * R])
    row0, row1 = call(
        first_rows_kernel, (out(R, 9 * R), out(R, 8 * R)), (x_head, bases, white_noise), flops=6 * leaf * R * 17 * R
    )
    got0 = swap(row0, CORE_MASK)
    got1 = swap(row1, CORE_MASK)
    x_second, keep2, send2 = call(
        second_rows_kernel,
        (out(leaf, R), out(HALF, 7 * R), out(HALF, 7 * R)),
        (leaf_inverse, bases, white_noise),
        index=index,
        flops=6 * leaf * R * (leaf + 7 * R),
    )
    got2 = swap(send2, CORE_MASK)
    weights = []
    panel, w = invert(0, row0, got0, index)
    weights.append(w)
    row1, half, half2 = call(
        row1_kernel,
        (out(R, 8 * R), out(HALF, 8 * R), out(HALF, 7 * R)),
        (row1, got1, keep2, got2, panel, w),
        index=index,
        flops=90 * R**3,
    )
    got = swap(half, 2)
    (x_tail,) = call(
        tail_solve_kernel,
        (out(leaf, 6 * R),),
        (leaf_inverse, bases, white_noise),
        scratch=(pltpu.VMEM((leaf, 6 * R), jnp.bfloat16),) * 2,
        flops=6 * leaf * leaf * 6 * R,
    )
    width3 = row_blocks(3)[1]
    keep, send = call(
        rest_rows_kernel,
        (out(HALF, width3), out(HALF, width3)),
        (bases, x_tail),
        index=index,
        flops=6 * leaf * R * width3,
    )
    got_rest = swap(send, CORE_MASK)
    (rest,) = call(rest0_kernel, (out(HALF, width3),), (keep, got_rest, panel, w), index=index, flops=update_flops(2))
    half2_after, got = lax.optimization_barrier((half2, got))
    got2 = swap(half2_after, 2)
    half = half + got
    panel, w = invert(1, half, swap(half, CORE_MASK), index)
    weights.append(w)
    (half,) = call(ahead_kernel, (out(HALF, 7 * R),), (half2, got2, panel, w), index=index, flops=42 * R**3)
    got = swap(half, 4)
    quarters = call(
        update1_kernel,
        (out(QUARTER, width3),) * 4,
        (rest, row1, w),
        index=index,
        scratch=(pltpu.VMEM((R, width3), F32),),
        flops=update_flops(2),
    )
    quarters, got = lax.optimization_barrier((quarters, got))
    half = half + got
    panel, w = invert(2, half, swap(half, CORE_MASK), index)
    weights.append(w)
    rest = quarters[0]
    for mask, part in zip(RING_MASKS, quarters[1:]):
        rest = rest + swap(part, mask)
    for level in range(2, 6):
        width = (LEVELS + 1 - level) * R
        if level > 2:
            rest = rest + swap(rest, 1 << level)
            if level < 5:
                row = ring_all(rest[:, :width])
            else:
                rest = ring_all(rest)
                row = rest[:, :, :width]
            panel, w = invert(level, row, swap(row, CORE_MASK), index)
            weights.append(w)
        next_width = row_blocks(level + 1)[1]
        if level < 5:
            (rest,) = call(
                update_quarter_kernel(level),
                (out(QUARTER, next_width),),
                (rest, panel, w),
                index=index,
                scratch=(pltpu.VMEM((R, next_width), F32),),
                flops=update_flops(level),
            )
        else:
            half, rest = call(
                update5_kernel,
                (out(HALF, 3 * R), out(HALF, 2 * R)),
                (rest, panel, w),
                index=index,
                scratch=(pltpu.VMEM((HALF, 9 * R), F32),),
                flops=update_flops(level),
            )
        if level == 3:
            t = [None, None, None, w]
            for j in (2, 1, 0):
                below = jnp.concatenate(t[j + 1 :], axis=0)
                mid = (3 - j) * R
                t[j] = weights[j][:, mid:] - high_dot(weights[j][:, :mid], below)
            coeffs = jnp.concatenate(t, axis=0)
            heads = (
                high_dot(x_head, coeffs[: 2 * R])
                + high_dot(x_second, coeffs[2 * R : 3 * R])
                + high_dot(x_tail[:, :R], coeffs[3 * R :])
            )
            solved = x_tail[:, R:] - heads
        elif level > 3:
            solved = solved[:, R:] - high_dot(solved[:, :R], w)
    got, got_rest = swap(half, 64), swap(rest, 64)
    half = half + got
    panel, w = invert(6, half, swap(half, CORE_MASK), index)
    solved = solved[:, R:] - high_dot(solved[:, :R], w)
    (half,) = call(update6_kernel, (out(HALF, 2 * R),), (rest, got_rest, panel, w), index=index, flops=update_flops(6))
    half = half + swap(half, 128)
    _, w = invert(7, half, swap(half, CORE_MASK), index)
    (answer,) = call(last_kernel, (out(solved.shape[0], R),), (solved, w), flops=6 * solved.shape[0] * R * R)
    return answer


def solution(mesh):
    in_specs = (P("leaf", None), P("leaf", None), P("leaf", None))
    out_specs = P("leaf", None)
    return jax.shard_map(tree_solve, mesh=mesh, in_specs=in_specs, out_specs=out_specs, check_vma=False)
```

```python
import jax
import jax.numpy as jnp
from jax import lax
from jax.experimental import pallas as pl
from jax.experimental.pallas import tpu as pltpu
from jax.sharding import PartitionSpec as P


R = 128
HALF = R // 2
QUARTER = HALF // 4
LEVELS = 8
F32 = jnp.float32
CORE_MASK = 1
TURNS = 8
RING_MASKS = (2, 4, 6)


def swap(value, mask):
    return lax.ppermute(value, "leaf", [(i, i ^ mask) for i in range(lax.axis_size("leaf"))])


def split(v):
    high = v.astype(jnp.bfloat16)
    return high, (v - high.astype(F32)).astype(jnp.bfloat16)


def dot_split(a, b, contract=(1, 0)):
    dims = (((contract[0],), (contract[1],)), ((), ()))

    def one(p, q):
        return lax.dot_general(p, q, dims, preferred_element_type=F32)

    return one(a[0], b[0]) + (one(a[0], b[1]) + one(a[1], b[0]))


def cols(parts, start, stop):
    return tuple(part[:, start:stop] for part in parts)


def row_blocks(first):
    offset = 0
    out = []
    for m in range(first, LEVELS):
        width = (LEVELS + 1 - m) * R
        out.append((m, offset, width))
        offset += width
    return out, offset


def spd_inverse(rows):
    shape = (8, R)
    sub = lax.broadcasted_iota(jnp.int32, shape, 0)
    lane = lax.broadcasted_iota(jnp.int32, shape, 1)

    def spread_row(v, i):
        return jnp.broadcast_to(v[i : i + 1, :], shape)

    def spread_col(v, k):
        return jnp.broadcast_to(v[:, k : k + 1], shape)

    count = R // 8
    turns = TURNS
    per_turn = count // turns

    def eliminate(rows, p):
        rows = list(rows)
        panel = rows[p]
        base = 8 * p
        panel_rows = [spread_row(panel, j) for j in range(8)]
        d = [spread_col(panel, base + j) for j in range(8)]
        for a in range(0, 8, 2):
            b = a + 1
            ra = [spread_row(d[j], a) for j in range(8)]
            rb = [spread_row(d[j], b) for j in range(8)]
            inv_det = 1.0 / (ra[a] * rb[b] - ra[b] * rb[a])
            ma, mb = sub == a, sub == b
            ca, cb = d[a], d[b]
            ta = (ca * rb[b] - cb * rb[a]) * inv_det
            tb = (cb * ra[a] - ca * ra[b]) * inv_det
            iaa, iab = rb[b] * inv_det, -(ra[b] * inv_det)
            iba, ibb = -(rb[a] * inv_det), ra[a] * inv_det
            for j in range(8):
                if j == a:
                    d[j] = jnp.where(ma, iaa, jnp.where(mb, iba, -ta))
                elif j == b:
                    d[j] = jnp.where(ma, iab, jnp.where(mb, ibb, -tb))
                else:
                    na = iaa * ra[j] + iab * rb[j]
                    nb = iba * ra[j] + ibb * rb[j]
                    d[j] = jnp.where(ma, na, jnp.where(mb, nb, d[j] - (ta * ra[j] + tb * rb[j])))
        inside = (lane >= base) & (lane < base + 8)
        panel = None
        for j in range(8):
            term = d[j] * jnp.where(inside, jnp.where(lane == base + j, 1.0, 0.0), panel_rows[j])
            panel = term if panel is None else panel + term
        rows[p] = panel
        spread = [spread_row(panel, j) for j in range(8)]
        for step in range(1, count):
            i = (p + step) % count
            c = rows[i]
            total = None
            for j in range(0, 8, 2):
                pair = spread_col(c, base + j) * spread[j] + spread_col(c, base + j + 1) * spread[j + 1]
                total = pair if total is None else total + pair
            rows[i] = jnp.where(inside, 0.0, c) - total
        return rows

    def turn(_, rows):
        for p in range(per_turn):
            rows = eliminate(rows, p)
        rows = rows[per_turn:] + rows[:per_turn]
        return tuple(pltpu.roll(row, R - 8 * per_turn, 1) for row in rows)

    return list(lax.fori_loop(0, turns, turn, tuple(rows)))


def vmem(n):
    return [pl.BlockSpec(memory_space=pltpu.VMEM)] * n


def smem():
    return [pl.BlockSpec(memory_space=pltpu.SMEM)]


def out(*shape):
    return jax.ShapeDtypeStruct(shape, F32)


def call(kernel, outs, args, index=None, scratch=(), flops=0):
    moved = 4 * (sum(a.size for a in args) + sum(o.size for o in outs))
    head = [] if index is None else [index]
    return pl.pallas_call(
        kernel,
        out_shape=outs,
        in_specs=(smem() if head else []) + vmem(len(args)),
        out_specs=vmem(len(outs)),
        scratch_shapes=list(scratch),
        cost_estimate=pl.CostEstimate(flops=flops, bytes_accessed=moved, transcendentals=0),
        compiler_params=pltpu.CompilerParams(vmem_limit_bytes=16 << 20),
    )(*head, *args)


HEAD = 3 * R
CHUNK = 256


def head_kernel(
    index_ref, a_hbm, u_hbm, w_hbm, x_ref, rows_ref, keep_ref, send_ref, a, u, w, u_high, u_low, row2, a_sem, sem
):
    core = index_ref[0] & 1
    chunks = a.shape[0]
    copies = [
        pltpu.make_async_copy(u_hbm.at[:, :HEAD], u.at[:, :HEAD], sem.at[0]),
        pltpu.make_async_copy(u_hbm.at[:, HEAD:], u.at[:, HEAD:], sem.at[1]),
        pltpu.make_async_copy(w_hbm, w, sem.at[2]),
    ]

    def a_copy(r):
        return pltpu.make_async_copy(a_hbm.at[pl.ds(r * CHUNK, CHUNK), :], a.at[r], a_sem.at[r])

    copies[0].start()
    a_copy(0).start()
    copies[1].start()
    copies[2].start()
    for r in range(1, chunks):
        a_copy(r).start()
    copies[0].wait()
    u_high[...], u_low[...] = split(u[:, :HEAD])
    rows_ref[...] = jnp.zeros_like(rows_ref)
    row2[...] = jnp.zeros_like(row2)

    @pl.loop(0, chunks)
    def _(r):
        a_copy(r).wait()
        span = pl.ds(pl.multiple_of(r * CHUNK, CHUNK), CHUNK)
        x = dot_split(split(a[r]), (u_high[...], u_low[...]))
        x_ref[span, :] = x

        @pl.when(r == 0)
        def _():
            copies[1].wait()
            copies[2].wait()

        x = split(x)
        chunk_u, chunk_w = split(u[span, :]), split(w[span, :])
        at = 0
        for m in range(3):
            left = cols(x, m * R, (m + 1) * R)
            width = (LEVELS - m) * R
            piece = dot_split(left, cols(chunk_u, m * R, LEVELS * R), (0, 0))
            noise = dot_split(left, chunk_w, (0, 0))
            if m < 2:
                rows_ref[:, at : at + width] += piece
                rows_ref[:, at + width : at + width + R] += noise
                at += width + R
            else:
                row2[:, :width] += piece
                row2[:, width:] += noise

    keep_ref[...] = jnp.where(core == 0, row2[:HALF, :], row2[HALF:, :])
    send_ref[...] = jnp.where(core == 0, row2[HALF:, :], row2[:HALF, :])


def head(index, leaf_inverse, bases, white_noise):
    leaf = leaf_inverse.shape[0]
    n2 = (LEVELS - 1) * R
    return pl.pallas_call(
        head_kernel,
        name="head",
        out_shape=(out(leaf, HEAD), out(R, 17 * R), out(HALF, n2), out(HALF, n2)),
        in_specs=smem() + [pl.BlockSpec(memory_space=pltpu.HBM)] * 3,
        out_specs=vmem(4),
        scratch_shapes=[
            pltpu.VMEM((leaf // CHUNK, CHUNK, leaf), F32),
            pltpu.VMEM((leaf, LEVELS * R), F32),
            pltpu.VMEM((leaf, R), F32),
            pltpu.VMEM((leaf, HEAD), jnp.bfloat16),
            pltpu.VMEM((leaf, HEAD), jnp.bfloat16),
            pltpu.VMEM((R, n2), F32),
            pltpu.SemaphoreType.DMA((leaf // CHUNK,)),
            pltpu.SemaphoreType.DMA((3,)),
        ],
        cost_estimate=pl.CostEstimate(flops=6 * leaf * R * 54 * R, bytes_accessed=8 * leaf * leaf, transcendentals=0),
        compiler_params=pltpu.CompilerParams(vmem_limit_bytes=24 << 20),
    )(index, leaf_inverse, bases, white_noise)


def tail_solve_kernel(a_ref, u_ref, w_ref, x_ref, high_ref, low_ref):
    tail = (LEVELS - 3) * R
    high_ref[:, :tail], low_ref[:, :tail] = split(u_ref[:, 3 * R :])
    high_ref[:, tail:], low_ref[:, tail:] = split(w_ref[...])

    @pl.loop(0, 4)
    def _(r):
        rows = pl.ds(pl.multiple_of(r * 2 * R, 2 * R), 2 * R)
        x_ref[rows, :] = dot_split(split(a_ref[rows, :]), (high_ref[...], low_ref[...]))


def rest_rows_kernel(index_ref, u_ref, x_ref, keep_ref, send_ref):
    core = index_ref[0] & 1
    x = split(x_ref[...])
    for m, at, width in row_blocks(3)[0]:
        u = split(u_ref[:, m * R : (m + 1) * R])
        piece = dot_split(u, cols(x, (m - 3) * R, (LEVELS - 2) * R), (0, 0))
        keep_ref[:, at : at + width] = jnp.where(core == 0, piece[:HALF], piece[HALF:])
        send_ref[:, at : at + width] = jnp.where(core == 0, piece[HALF:], piece[:HALF])


def invert_store(panel_ref, w_ref):
    rows = [panel_ref[8 * i : 8 * i + 8, :R] for i in range(R // 8)]
    sub = lax.broadcasted_iota(jnp.int32, (8, R), 0)
    lane = lax.broadcasted_iota(jnp.int32, (8, R), 1)
    rows = [row + jnp.where(lane == sub + 8 * i, 1.0, 0.0) for i, row in enumerate(rows)]
    inverse = split(jnp.concatenate(spd_inverse(rows), axis=0))
    w_ref[...] = dot_split(inverse, split(panel_ref[:, R:]))


def invert_sum_kernel(own_ref, got_ref, panel_ref, w_ref):
    n = panel_ref.shape[1]
    panel_ref[...] = own_ref[:, :n] + got_ref[:, :n]
    invert_store(panel_ref, w_ref)


def invert_half_kernel(index_ref, own_ref, got_ref, panel_ref, w_ref):
    core = index_ref[0] & 1
    own, got = own_ref[...], got_ref[...]
    panel_ref[:HALF, :] = jnp.where(core == 0, own, got)
    panel_ref[HALF:, :] = jnp.where(core == 0, got, own)
    invert_store(panel_ref, w_ref)


def invert_ring_kernel(index_ref, own_ref, got_ref, panel_ref, w_ref):
    core = index_ref[0] & 1
    x = (index_ref[0] >> 1) & 3
    for k in range(4):
        at = QUARTER * jnp.bitwise_xor(x, k)
        mine = pl.multiple_of(core * HALF + at, QUARTER)
        other = pl.multiple_of((1 - core) * HALF + at, QUARTER)
        panel_ref[pl.ds(mine, QUARTER), :] = own_ref[k]
        panel_ref[pl.ds(other, QUARTER), :] = got_ref[k]
    invert_store(panel_ref, w_ref)


def invert(level, own, got, index):
    n = (LEVELS + 1 - level) * R
    outs = (out(R, n), out(R, n - R))
    flops = 6 * R * R * n + 2 * R * R * R * 40
    if level == 0:
        return call(invert_sum_kernel, outs, (own, got), flops=flops)
    kernel = invert_ring_kernel if 3 <= level <= 5 else invert_half_kernel
    return call(kernel, outs, (own, got), index=index, flops=flops)


def row1_kernel(index_ref, own_ref, got_ref, keep_ref, got2_ref, panel_ref, w_ref, row_ref, half_ref, half2_ref):
    core = index_ref[0] & 1
    w = split(w_ref[...])
    row = own_ref[:, 9 * R :] + got_ref[:, 9 * R :] - dot_split(split(panel_ref[:, R : 2 * R]), w, (0, 0))
    row_ref[...] = row
    half_ref[...] = jnp.where(core == 0, row[:HALF], row[HALF:])
    change = dot_split(split(panel_ref[:, 2 * R : 3 * R]), cols(w, R, LEVELS * R), (0, 0))
    half2_ref[...] = keep_ref[...] + got2_ref[...] - jnp.where(core == 0, change[:HALF], change[HALF:])


def ahead_kernel(index_ref, own_ref, got_ref, panel_ref, w_ref, half_ref):
    core = index_ref[0] & 1
    change = dot_split(split(panel_ref[:, R : 2 * R]), split(w_ref[...]), (0, 0))
    half_ref[...] = own_ref[...] + got_ref[...] - jnp.where(core == 0, change[:HALF], change[HALF:])


def downdate(core, level, panel_ref, w_ref, rows):
    w = split(w_ref[...])
    for m, offset, width in rows:
        left = split(panel_ref[:, (m - level) * R : (m - level + 1) * R])
        full = dot_split(left, cols(w, (m - level - 1) * R, (LEVELS - level) * R), (0, 0))
        yield m, offset, width, jnp.where(core == 0, full[:HALF], full[HALF:])


def rest0_kernel(index_ref, own_ref, got_ref, panel_ref, w_ref, rest_ref):
    core = index_ref[0] & 1
    for m, at, width, change in downdate(core, 0, panel_ref, w_ref, row_blocks(3)[0]):
        span = slice(at, at + width)
        rest_ref[:, span] = own_ref[:, span] + got_ref[:, span] - change


def whole_downdate(level, panel_ref, w_ref, rows, scr):
    w = split(w_ref[...])
    for m, at, width in rows:
        left = split(panel_ref[:, (m - level) * R : (m - level + 1) * R])
        scr[:, at : at + width] = dot_split(left, cols(w, (m - level - 1) * R, (LEVELS - level) * R), (0, 0))


def quarter_at(index_ref, k):
    x = (index_ref[0] >> 1) & 3
    return QUARTER * jnp.bitwise_xor(x, k)


def update1_kernel(index_ref, rest_ref, panel_ref, w_ref, q0, q1, q2, q3, scr):
    core = index_ref[0] & 1
    whole_downdate(1, panel_ref, w_ref, row_blocks(3)[0], scr)
    for k, q in enumerate((q0, q1, q2, q3)):
        at = quarter_at(index_ref, k)
        mine = pl.multiple_of(at, QUARTER)
        both = pl.multiple_of(core * HALF + at, QUARTER)
        q[...] = rest_ref[pl.ds(mine, QUARTER), :] - scr[pl.ds(both, QUARTER), :]


def update_quarter_kernel(level):
    skip = (LEVELS + 1 - level) * R if level > 2 else 0

    def kernel(index_ref, rest_ref, panel_ref, w_ref, out_ref, scr):
        core = index_ref[0] & 1
        whole_downdate(level, panel_ref, w_ref, row_blocks(level + 1)[0], scr)
        at = pl.multiple_of(core * HALF + quarter_at(index_ref, 0), QUARTER)
        out_ref[...] = rest_ref[:, skip:] - scr[pl.ds(at, QUARTER), :]

    return kernel


def store_next(level, m, at, value, row_ref, rest_ref):
    if m == level + 1:
        row_ref[...] = value
    else:
        at -= (LEVELS - level) * R
        rest_ref[:, at : at + value.shape[1]] = value


def update5_kernel(index_ref, own_ref, panel_ref, w_ref, row_ref, rest_ref, scr):
    core = index_ref[0] & 1
    for k in range(4):
        at = pl.multiple_of(quarter_at(index_ref, k), QUARTER)
        scr[pl.ds(at, QUARTER), :] = own_ref[k]
    skip = (LEVELS + 1 - 5) * R
    for m, at, width, change in downdate(core, 5, panel_ref, w_ref, row_blocks(6)[0]):
        store_next(5, m, at, scr[:, skip + at : skip + at + width] - change, row_ref, rest_ref)


def update6_kernel(index_ref, own_ref, got_ref, panel_ref, w_ref, row_ref):
    core = index_ref[0] & 1
    for _, _, _, change in downdate(core, 6, panel_ref, w_ref, row_blocks(7)[0]):
        row_ref[...] = own_ref[...] + got_ref[...] - change


def solve_step_kernel(solved_ref, w_ref, next_ref):
    w = split(w_ref[...])

    @pl.loop(0, solved_ref.shape[0] // CHUNK)
    def _(r):
        span = pl.ds(pl.multiple_of(r * CHUNK, CHUNK), CHUNK)
        next_ref[span, :] = solved_ref[span, R:] - dot_split(split(solved_ref[span, :R]), w)


def solve_step(solved, w):
    rows, n = solved.shape[0], solved.shape[1] - R
    (result,) = call(solve_step_kernel, (out(rows, n),), (solved, w), flops=6 * rows * R * n)
    return result


def solve_four_kernel(head_ref, tail_ref, w0, w1, w2, w3, next_ref, high, low):
    for j, w in ((3, w3), (2, w2), (1, w1), (0, w0)):
        mid = (3 - j) * R
        t = w[:, mid:]
        if j < 3:
            below = slice((j + 1) * R, 4 * R)
            t = t - dot_split(split(w[:, :mid]), (high[below, :], low[below, :]))
        high[j * R : (j + 1) * R, :], low[j * R : (j + 1) * R, :] = split(t)

    @pl.loop(0, head_ref.shape[0] // CHUNK)
    def _(r):
        span = pl.ds(pl.multiple_of(r * CHUNK, CHUNK), CHUNK)
        change = dot_split(split(head_ref[span, :]), (high[:HEAD, :], low[:HEAD, :]))
        change = change + dot_split(split(tail_ref[span, :R]), (high[HEAD:, :], low[HEAD:, :]))
        next_ref[span, :] = tail_ref[span, R:] - change


def update_flops(level):
    return sum(6 * R * R * width for _, _, width in row_blocks(level + 1)[0])


def ring_all(value):
    return jnp.stack([value] + [swap(value, mask) for mask in RING_MASKS])


def tree_solve(white_noise, leaf_inverse, bases):
    index = lax.axis_index("leaf").astype(jnp.int32).reshape(1)
    leaf = leaf_inverse.shape[0]
    x_head, rows01, keep2, send2 = head(index, leaf_inverse, bases, white_noise)
    got01 = swap(rows01, CORE_MASK)
    got2 = swap(send2, CORE_MASK)
    weights = []
    panel, w = invert(0, rows01, got01, index)
    weights.append(w)
    row1, half, half2 = call(
        row1_kernel,
        (out(R, 8 * R), out(HALF, 8 * R), out(HALF, 7 * R)),
        (rows01, got01, keep2, got2, panel, w),
        index=index,
        flops=90 * R**3,
    )
    got = swap(half, 2)
    (x_tail,) = call(
        tail_solve_kernel,
        (out(leaf, 6 * R),),
        (leaf_inverse, bases, white_noise),
        scratch=(pltpu.VMEM((leaf, 6 * R), jnp.bfloat16),) * 2,
        flops=6 * leaf * leaf * 6 * R,
    )
    width3 = row_blocks(3)[1]
    keep, send = call(
        rest_rows_kernel,
        (out(HALF, width3), out(HALF, width3)),
        (bases, x_tail),
        index=index,
        flops=6 * leaf * R * width3,
    )
    got_rest = swap(send, CORE_MASK)
    (rest,) = call(rest0_kernel, (out(HALF, width3),), (keep, got_rest, panel, w), index=index, flops=update_flops(2))
    half2_after, got = lax.optimization_barrier((half2, got))
    got2 = swap(half2_after, 2)
    half = half + got
    panel, w = invert(1, half, swap(half, CORE_MASK), index)
    weights.append(w)
    (half,) = call(ahead_kernel, (out(HALF, 7 * R),), (half2, got2, panel, w), index=index, flops=42 * R**3)
    got = swap(half, 4)
    quarters = call(
        update1_kernel,
        (out(QUARTER, width3),) * 4,
        (rest, row1, w),
        index=index,
        scratch=(pltpu.VMEM((R, width3), F32),),
        flops=update_flops(2),
    )
    quarters, got = lax.optimization_barrier((quarters, got))
    half = half + got
    other = swap(half, CORE_MASK)
    panel, w = invert(2, half, other, index)
    weights.append(w)
    rest = quarters[0]
    for k in (1, 2, 0):
        part = swap(quarters[1 + k], RING_MASKS[k])
        rest = rest + part
    for level in range(2, 6):
        width = (LEVELS + 1 - level) * R
        if level > 2:
            rest = rest + swap(rest, 1 << level)
            if level < 5:
                row = ring_all(rest[:, :width])
            else:
                rest = ring_all(rest)
                row = rest[:, :, :width]
            panel, w = invert(level, row, swap(row, CORE_MASK), index)
            weights.append(w)
        next_width = row_blocks(level + 1)[1]
        if level < 5:
            (rest,) = call(
                update_quarter_kernel(level),
                (out(QUARTER, next_width),),
                (rest, panel, w),
                index=index,
                scratch=(pltpu.VMEM((R, next_width), F32),),
                flops=update_flops(level),
            )
        else:
            half, rest = call(
                update5_kernel,
                (out(HALF, 3 * R), out(HALF, 2 * R)),
                (rest, panel, w),
                index=index,
                scratch=(pltpu.VMEM((HALF, 9 * R), F32),),
                flops=update_flops(level),
            )
        if level == 3:
            (solved,) = call(
                solve_four_kernel,
                (out(leaf, 5 * R),),
                (x_head, x_tail, *weights),
                scratch=(pltpu.VMEM((4 * R, 5 * R), jnp.bfloat16),) * 2,
                flops=6 * leaf * 4 * R * 5 * R,
            )
        elif level > 3:
            solved = solve_step(solved, w)
    got, got_rest = swap(half, 64), swap(rest, 64)
    half = half + got
    panel, w = invert(6, half, swap(half, CORE_MASK), index)
    solved = solve_step(solved, w)
    (half,) = call(update6_kernel, (out(HALF, 2 * R),), (rest, got_rest, panel, w), index=index, flops=update_flops(6))
    half = half + swap(half, 128)
    _, w = invert(7, half, swap(half, CORE_MASK), index)
    return solve_step(solved, w)


def solution(mesh):
    in_specs = (P("leaf", None), P("leaf", None), P("leaf", None))
    out_specs = P("leaf", None)
    return jax.shard_map(tree_solve, mesh=mesh, in_specs=in_specs, out_specs=out_specs, check_vma=False)
```

```python
import jax
import jax.numpy as jnp
from jax import lax
from jax.experimental import pallas as pl
from jax.experimental.pallas import tpu as pltpu
from jax.sharding import PartitionSpec as P


R = 128
HALF = R // 2
QUARTER = HALF // 4
LEVELS = 8
F32 = jnp.float32
CORE_MASK = 1
TURNS = 4
RING_MASKS = (2, 4, 6)


def swap(value, mask):
    return lax.ppermute(value, "leaf", [(i, i ^ mask) for i in range(lax.axis_size("leaf"))])


def split(v):
    high = v.astype(jnp.bfloat16)
    return high, (v - high.astype(F32)).astype(jnp.bfloat16)


def dot_split(a, b, contract=(1, 0)):
    dims = (((contract[0],), (contract[1],)), ((), ()))

    def one(p, q):
        return lax.dot_general(p, q, dims, preferred_element_type=F32)

    return one(a[0], b[0]) + (one(a[0], b[1]) + one(a[1], b[0]))


def cols(parts, start, stop):
    return tuple(part[:, start:stop] for part in parts)


def row_blocks(first):
    offset = 0
    out = []
    for m in range(first, LEVELS):
        width = (LEVELS + 1 - m) * R
        out.append((m, offset, width))
        offset += width
    return out, offset


def spd_inverse(rows):
    shape = (8, R)
    sub = lax.broadcasted_iota(jnp.int32, shape, 0)
    lane = lax.broadcasted_iota(jnp.int32, shape, 1)

    def spread_row(v, i):
        return jnp.broadcast_to(v[i : i + 1, :], shape)

    def spread_col(v, k):
        return jnp.broadcast_to(v[:, k : k + 1], shape)

    count = R // 8
    turns = TURNS
    per_turn = count // turns

    def add_up(terms):
        while len(terms) > 1:
            terms = [a + b for a, b in zip(terms[::2], terms[1::2])]
        return terms[0]

    def eliminate(rows, p):
        base = 8 * p
        panel_rows = [spread_row(rows[p], j) for j in range(8)]
        d = [spread_col(rows[p], base + j) for j in range(8)]
        for a in range(0, 8, 2):
            b = a + 1
            ra = [spread_row(d[j], a) for j in range(8)]
            rb = [spread_row(d[j], b) for j in range(8)]
            inv_det = 1.0 / (ra[a] * rb[b] - ra[b] * rb[a])
            ma, mb = sub == a, sub == b
            va = jnp.where(ma, -rb[b], jnp.where(mb, rb[a], d[a] * rb[b] - d[b] * rb[a]))
            vb = jnp.where(ma, ra[b], jnp.where(mb, -ra[a], d[b] * ra[a] - d[a] * ra[b]))
            for j in range(8):
                if j == a:
                    d[j] = -(va * inv_det)
                elif j == b:
                    d[j] = -(vb * inv_det)
                else:
                    d[j] = jnp.where(ma | mb, 0.0, d[j]) - (va * ra[j] + vb * rb[j]) * inv_det
        inside = (lane >= base) & (lane < base + 8)
        panel = add_up(
            [d[j] * jnp.where(inside, jnp.where(lane == base + j, 1.0, 0.0), panel_rows[j]) for j in range(8)]
        )
        after = (p + 1) % count
        ahead = add_up([spread_col(rows[after], base + j) * spread_row(panel, j) for j in range(8)])
        ahead = jnp.where(inside, 0.0, rows[after]) - ahead
        zeros = [jnp.zeros((8, R), F32)]
        pivot_rows = jnp.concatenate(zeros * p + [panel] + zeros * (count - 1 - p), axis=0)
        change = dot_split(split(jnp.concatenate(rows, axis=0)), split(pivot_rows))
        result = [jnp.where(inside, 0.0, row) - change[8 * i : 8 * i + 8, :] for i, row in enumerate(rows)]
        result[p], result[after] = panel, ahead
        return result

    def turn(_, rows):
        rows = list(rows)
        for p in range(per_turn):
            rows = eliminate(rows, p)
        rows = rows[per_turn:] + rows[:per_turn]
        return tuple(pltpu.roll(row, R - 8 * per_turn, 1) for row in rows)

    return list(lax.fori_loop(0, turns, turn, tuple(rows)))


def vmem(n):
    return [pl.BlockSpec(memory_space=pltpu.VMEM)] * n


def smem():
    return [pl.BlockSpec(memory_space=pltpu.SMEM)]


def out(*shape):
    return jax.ShapeDtypeStruct(shape, F32)


def call(kernel, outs, args, index=None, scratch=(), flops=0):
    moved = 4 * (sum(a.size for a in args) + sum(o.size for o in outs))
    head = [] if index is None else [index]
    return pl.pallas_call(
        kernel,
        out_shape=outs,
        in_specs=(smem() if head else []) + vmem(len(args)),
        out_specs=vmem(len(outs)),
        scratch_shapes=list(scratch),
        cost_estimate=pl.CostEstimate(flops=flops, bytes_accessed=moved, transcendentals=0),
        compiler_params=pltpu.CompilerParams(vmem_limit_bytes=16 << 20),
    )(*head, *args)


HEAD = 3 * R
CHUNK = 256


def head_kernel(
    index_ref, a_hbm, u_hbm, w_hbm, x_ref, rows_ref, keep_ref, send_ref, a, u, w, u_high, u_low, row2, a_sem, sem
):
    core = index_ref[0] & 1
    chunks = a.shape[0]
    copies = [
        pltpu.make_async_copy(u_hbm.at[:, :HEAD], u.at[:, :HEAD], sem.at[0]),
        pltpu.make_async_copy(u_hbm.at[:, HEAD:], u.at[:, HEAD:], sem.at[1]),
        pltpu.make_async_copy(w_hbm, w, sem.at[2]),
    ]

    def a_copy(r):
        return pltpu.make_async_copy(a_hbm.at[pl.ds(r * CHUNK, CHUNK), :], a.at[r], a_sem.at[r])

    copies[0].start()
    a_copy(0).start()
    copies[1].start()
    copies[2].start()
    for r in range(1, chunks):
        a_copy(r).start()
    copies[0].wait()
    u_high[...], u_low[...] = split(u[:, :HEAD])
    rows_ref[...] = jnp.zeros_like(rows_ref)
    row2[...] = jnp.zeros_like(row2)

    @pl.loop(0, chunks)
    def _(r):
        a_copy(r).wait()
        span = pl.ds(pl.multiple_of(r * CHUNK, CHUNK), CHUNK)
        x = dot_split(split(a[r]), (u_high[...], u_low[...]))
        x_ref[span, :] = x

        @pl.when(r == 0)
        def _():
            copies[1].wait()
            copies[2].wait()

        x = split(x)
        chunk_u, chunk_w = split(u[span, :]), split(w[span, :])
        at = 0
        for m in range(3):
            left = cols(x, m * R, (m + 1) * R)
            width = (LEVELS - m) * R
            piece = dot_split(left, cols(chunk_u, m * R, LEVELS * R), (0, 0))
            noise = dot_split(left, chunk_w, (0, 0))
            if m < 2:
                rows_ref[:, at : at + width] += piece
                rows_ref[:, at + width : at + width + R] += noise
                at += width + R
            else:
                row2[:, :width] += piece
                row2[:, width:] += noise

    keep_ref[...] = jnp.where(core == 0, row2[:HALF, :], row2[HALF:, :])
    send_ref[...] = jnp.where(core == 0, row2[HALF:, :], row2[:HALF, :])


def head(index, leaf_inverse, bases, white_noise):
    leaf = leaf_inverse.shape[0]
    n2 = (LEVELS - 1) * R
    return pl.pallas_call(
        head_kernel,
        name="head",
        out_shape=(out(leaf, HEAD), out(R, 17 * R), out(HALF, n2), out(HALF, n2)),
        in_specs=smem() + [pl.BlockSpec(memory_space=pltpu.HBM)] * 3,
        out_specs=vmem(4),
        scratch_shapes=[
            pltpu.VMEM((leaf // CHUNK, CHUNK, leaf), F32),
            pltpu.VMEM((leaf, LEVELS * R), F32),
            pltpu.VMEM((leaf, R), F32),
            pltpu.VMEM((leaf, HEAD), jnp.bfloat16),
            pltpu.VMEM((leaf, HEAD), jnp.bfloat16),
            pltpu.VMEM((R, n2), F32),
            pltpu.SemaphoreType.DMA((leaf // CHUNK,)),
            pltpu.SemaphoreType.DMA((3,)),
        ],
        cost_estimate=pl.CostEstimate(flops=6 * leaf * R * 54 * R, bytes_accessed=8 * leaf * leaf, transcendentals=0),
        compiler_params=pltpu.CompilerParams(vmem_limit_bytes=60 << 20),
    )(index, leaf_inverse, bases, white_noise)


def tail_solve_kernel(a_ref, u_ref, w_ref, x_ref, high_ref, low_ref):
    tail = (LEVELS - 3) * R
    high_ref[:, :tail], low_ref[:, :tail] = split(u_ref[:, 3 * R :])
    high_ref[:, tail:], low_ref[:, tail:] = split(w_ref[...])

    @pl.loop(0, 4)
    def _(r):
        rows = pl.ds(pl.multiple_of(r * 2 * R, 2 * R), 2 * R)
        x_ref[rows, :] = dot_split(split(a_ref[rows, :]), (high_ref[...], low_ref[...]))


def rest_rows_kernel(index_ref, u_ref, x_ref, keep_ref, send_ref):
    core = index_ref[0] & 1
    x = split(x_ref[...])
    for m, at, width in row_blocks(3)[0]:
        u = split(u_ref[:, m * R : (m + 1) * R])
        piece = dot_split(u, cols(x, (m - 3) * R, (LEVELS - 2) * R), (0, 0))
        keep_ref[:, at : at + width] = jnp.where(core == 0, piece[:HALF], piece[HALF:])
        send_ref[:, at : at + width] = jnp.where(core == 0, piece[HALF:], piece[:HALF])


def invert_store(panel_ref, w_ref):
    rows = [panel_ref[8 * i : 8 * i + 8, :R] for i in range(R // 8)]
    sub = lax.broadcasted_iota(jnp.int32, (8, R), 0)
    lane = lax.broadcasted_iota(jnp.int32, (8, R), 1)
    rows = [row + jnp.where(lane == sub + 8 * i, 1.0, 0.0) for i, row in enumerate(rows)]
    inverse = split(jnp.concatenate(spd_inverse(rows), axis=0))
    w_ref[...] = dot_split(inverse, split(panel_ref[:, R:]))


def invert_sum_kernel(own_ref, got_ref, panel_ref, w_ref):
    n = panel_ref.shape[1]
    panel_ref[...] = own_ref[:, :n] + got_ref[:, :n]
    invert_store(panel_ref, w_ref)


def invert_half_kernel(index_ref, own_ref, got_ref, panel_ref, w_ref):
    core = index_ref[0] & 1
    own, got = own_ref[...], got_ref[...]
    panel_ref[:HALF, :] = jnp.where(core == 0, own, got)
    panel_ref[HALF:, :] = jnp.where(core == 0, got, own)
    invert_store(panel_ref, w_ref)


def invert_ring_kernel(index_ref, own_ref, got_ref, panel_ref, w_ref):
    core = index_ref[0] & 1
    x = (index_ref[0] >> 1) & 3
    for k in range(4):
        at = QUARTER * jnp.bitwise_xor(x, k)
        mine = pl.multiple_of(core * HALF + at, QUARTER)
        other = pl.multiple_of((1 - core) * HALF + at, QUARTER)
        panel_ref[pl.ds(mine, QUARTER), :] = own_ref[k]
        panel_ref[pl.ds(other, QUARTER), :] = got_ref[k]
    invert_store(panel_ref, w_ref)


def invert(level, own, got, index):
    n = (LEVELS + 1 - level) * R
    outs = (out(R, n), out(R, n - R))
    flops = 6 * R * R * n + 2 * R * R * R * 40
    if level == 0:
        return call(invert_sum_kernel, outs, (own, got), flops=flops)
    kernel = invert_ring_kernel if 3 <= level <= 5 else invert_half_kernel
    return call(kernel, outs, (own, got), index=index, flops=flops)


def row1_kernel(index_ref, own_ref, got_ref, keep_ref, got2_ref, panel_ref, w_ref, row_ref, half_ref, half2_ref):
    core = index_ref[0] & 1
    w = split(w_ref[...])
    row = own_ref[:, 9 * R :] + got_ref[:, 9 * R :] - dot_split(split(panel_ref[:, R : 2 * R]), w, (0, 0))
    row_ref[...] = row
    half_ref[...] = jnp.where(core == 0, row[:HALF], row[HALF:])
    change = dot_split(split(panel_ref[:, 2 * R : 3 * R]), cols(w, R, LEVELS * R), (0, 0))
    half2_ref[...] = keep_ref[...] + got2_ref[...] - jnp.where(core == 0, change[:HALF], change[HALF:])


def ahead_kernel(index_ref, own_ref, got_ref, panel_ref, w_ref, half_ref):
    core = index_ref[0] & 1
    change = dot_split(split(panel_ref[:, R : 2 * R]), split(w_ref[...]), (0, 0))
    half_ref[...] = own_ref[...] + got_ref[...] - jnp.where(core == 0, change[:HALF], change[HALF:])


def downdate(core, level, panel_ref, w_ref, rows):
    w = split(w_ref[...])
    for m, offset, width in rows:
        left = split(panel_ref[:, (m - level) * R : (m - level + 1) * R])
        full = dot_split(left, cols(w, (m - level - 1) * R, (LEVELS - level) * R), (0, 0))
        yield m, offset, width, jnp.where(core == 0, full[:HALF], full[HALF:])


def rest0_kernel(index_ref, own_ref, got_ref, panel_ref, w_ref, rest_ref):
    core = index_ref[0] & 1
    for m, at, width, change in downdate(core, 0, panel_ref, w_ref, row_blocks(3)[0]):
        span = slice(at, at + width)
        rest_ref[:, span] = own_ref[:, span] + got_ref[:, span] - change


def whole_downdate(level, panel_ref, w_ref, rows, scr):
    w = split(w_ref[...])
    for m, at, width in rows:
        left = split(panel_ref[:, (m - level) * R : (m - level + 1) * R])
        scr[:, at : at + width] = dot_split(left, cols(w, (m - level - 1) * R, (LEVELS - level) * R), (0, 0))


def quarter_at(index_ref, k):
    x = (index_ref[0] >> 1) & 3
    return QUARTER * jnp.bitwise_xor(x, k)


def update1_kernel(index_ref, rest_ref, panel_ref, w_ref, q0, q1, q2, q3, scr):
    core = index_ref[0] & 1
    whole_downdate(1, panel_ref, w_ref, row_blocks(3)[0], scr)
    for k, q in enumerate((q0, q1, q2, q3)):
        at = quarter_at(index_ref, k)
        mine = pl.multiple_of(at, QUARTER)
        both = pl.multiple_of(core * HALF + at, QUARTER)
        q[...] = rest_ref[pl.ds(mine, QUARTER), :] - scr[pl.ds(both, QUARTER), :]


def update_quarter_kernel(level):
    skip = (LEVELS + 1 - level) * R if level > 2 else 0

    def kernel(index_ref, rest_ref, panel_ref, w_ref, out_ref, scr):
        core = index_ref[0] & 1
        whole_downdate(level, panel_ref, w_ref, row_blocks(level + 1)[0], scr)
        at = pl.multiple_of(core * HALF + quarter_at(index_ref, 0), QUARTER)
        out_ref[...] = rest_ref[:, skip:] - scr[pl.ds(at, QUARTER), :]

    return kernel


def store_next(level, m, at, value, row_ref, rest_ref):
    if m == level + 1:
        row_ref[...] = value
    else:
        at -= (LEVELS - level) * R
        rest_ref[:, at : at + value.shape[1]] = value


def update5_kernel(index_ref, own_ref, panel_ref, w_ref, row_ref, rest_ref, scr):
    core = index_ref[0] & 1
    for k in range(4):
        at = pl.multiple_of(quarter_at(index_ref, k), QUARTER)
        scr[pl.ds(at, QUARTER), :] = own_ref[k]
    skip = (LEVELS + 1 - 5) * R
    for m, at, width, change in downdate(core, 5, panel_ref, w_ref, row_blocks(6)[0]):
        store_next(5, m, at, scr[:, skip + at : skip + at + width] - change, row_ref, rest_ref)


def update6_kernel(index_ref, own_ref, got_ref, panel_ref, w_ref, row_ref):
    core = index_ref[0] & 1
    for _, _, _, change in downdate(core, 6, panel_ref, w_ref, row_blocks(7)[0]):
        row_ref[...] = own_ref[...] + got_ref[...] - change


def solve_step_kernel(solved_ref, w_ref, next_ref):
    w = split(w_ref[...])

    @pl.loop(0, solved_ref.shape[0] // CHUNK)
    def _(r):
        span = pl.ds(pl.multiple_of(r * CHUNK, CHUNK), CHUNK)
        next_ref[span, :] = solved_ref[span, R:] - dot_split(split(solved_ref[span, :R]), w)


def solve_step(solved, w):
    rows, n = solved.shape[0], solved.shape[1] - R
    (result,) = call(solve_step_kernel, (out(rows, n),), (solved, w), flops=6 * rows * R * n)
    return result


def solve_four_kernel(head_ref, tail_ref, w0, w1, w2, w3, next_ref, high, low):
    for j, w in ((3, w3), (2, w2), (1, w1), (0, w0)):
        mid = (3 - j) * R
        t = w[:, mid:]
        if j < 3:
            below = slice((j + 1) * R, 4 * R)
            t = t - dot_split(split(w[:, :mid]), (high[below, :], low[below, :]))
        high[j * R : (j + 1) * R, :], low[j * R : (j + 1) * R, :] = split(t)

    @pl.loop(0, head_ref.shape[0] // CHUNK)
    def _(r):
        span = pl.ds(pl.multiple_of(r * CHUNK, CHUNK), CHUNK)
        change = dot_split(split(head_ref[span, :]), (high[:HEAD, :], low[:HEAD, :]))
        change = change + dot_split(split(tail_ref[span, :R]), (high[HEAD:, :], low[HEAD:, :]))
        next_ref[span, :] = tail_ref[span, R:] - change


def update_flops(level):
    return sum(6 * R * R * width for _, _, width in row_blocks(level + 1)[0])


def ring_all(value):
    return jnp.stack([value] + [swap(value, mask) for mask in RING_MASKS])


def tree_solve(white_noise, leaf_inverse, bases):
    index = lax.axis_index("leaf").astype(jnp.int32).reshape(1)
    leaf = leaf_inverse.shape[0]
    x_head, rows01, keep2, send2 = head(index, leaf_inverse, bases, white_noise)
    got01 = swap(rows01, CORE_MASK)
    got2 = swap(send2, CORE_MASK)
    weights = []
    panel, w = invert(0, rows01, got01, index)
    weights.append(w)
    row1, half, half2 = call(
        row1_kernel,
        (out(R, 8 * R), out(HALF, 8 * R), out(HALF, 7 * R)),
        (rows01, got01, keep2, got2, panel, w),
        index=index,
        flops=90 * R**3,
    )
    got = swap(half, 2)
    (x_tail,) = call(
        tail_solve_kernel,
        (out(leaf, 6 * R),),
        (leaf_inverse, bases, white_noise),
        scratch=(pltpu.VMEM((leaf, 6 * R), jnp.bfloat16),) * 2,
        flops=6 * leaf * leaf * 6 * R,
    )
    width3 = row_blocks(3)[1]
    keep, send = call(
        rest_rows_kernel,
        (out(HALF, width3), out(HALF, width3)),
        (bases, x_tail),
        index=index,
        flops=6 * leaf * R * width3,
    )
    got_rest = swap(send, CORE_MASK)
    (rest,) = call(rest0_kernel, (out(HALF, width3),), (keep, got_rest, panel, w), index=index, flops=update_flops(2))
    half2_after, got = lax.optimization_barrier((half2, got))
    got2 = swap(half2_after, 2)
    half = half + got
    panel, w = invert(1, half, swap(half, CORE_MASK), index)
    weights.append(w)
    (half,) = call(ahead_kernel, (out(HALF, 7 * R),), (half2, got2, panel, w), index=index, flops=42 * R**3)
    got = swap(half, 4)
    quarters = call(
        update1_kernel,
        (out(QUARTER, width3),) * 4,
        (rest, row1, w),
        index=index,
        scratch=(pltpu.VMEM((R, width3), F32),),
        flops=update_flops(2),
    )
    half = half + got
    other = swap(half, CORE_MASK)
    panel, w = invert(2, half, other, index)
    weights.append(w)
    rest = quarters[0]
    for k in (1, 2, 0):
        part = swap(quarters[1 + k], RING_MASKS[k])
        rest = rest + part
    for level in range(2, 6):
        width = (LEVELS + 1 - level) * R
        if level > 2:
            got_rest = swap(rest, 1 << level)
            rest = rest + got_rest
            if level < 5:
                row = ring_all(rest[:, :width])
            else:
                rest = ring_all(rest)
                row = rest[:, :, :width]
            panel, w = invert(level, row, swap(row, CORE_MASK), index)
            weights.append(w)
        next_width = row_blocks(level + 1)[1]
        if level < 5:
            (rest,) = call(
                update_quarter_kernel(level),
                (out(QUARTER, next_width),),
                (rest, panel, w),
                index=index,
                scratch=(pltpu.VMEM((R, next_width), F32),),
                flops=update_flops(level),
            )
        else:
            half, rest = call(
                update5_kernel,
                (out(HALF, 3 * R), out(HALF, 2 * R)),
                (rest, panel, w),
                index=index,
                scratch=(pltpu.VMEM((HALF, 9 * R), F32),),
                flops=update_flops(level),
            )
        if level == 3:
            (solved,) = call(
                solve_four_kernel,
                (out(leaf, 5 * R),),
                (x_head, x_tail, *weights),
                scratch=(pltpu.VMEM((4 * R, 5 * R), jnp.bfloat16),) * 2,
                flops=6 * leaf * 4 * R * 5 * R,
            )
        elif level > 3:
            solved = solve_step(solved, w)
    got = swap(half, 64)
    got_rest = swap(rest, 64)
    half = half + got
    panel, w = invert(6, half, swap(half, CORE_MASK), index)
    solved = solve_step(solved, w)
    (half,) = call(update6_kernel, (out(HALF, 2 * R),), (rest, got_rest, panel, w), index=index, flops=update_flops(6))
    got = swap(half, 128)
    half = half + got
    _, w = invert(7, half, swap(half, CORE_MASK), index)
    return solve_step(solved, w)


def solution(mesh):
    in_specs = (P("leaf", None), P("leaf", None), P("leaf", None))
    out_specs = P("leaf", None)
    return jax.shard_map(tree_solve, mesh=mesh, in_specs=in_specs, out_specs=out_specs, check_vma=False)
```

```python
import jax
import jax.numpy as jnp
from jax import lax
from jax.experimental import pallas as pl
from jax.experimental.pallas import tpu as pltpu
from jax.sharding import PartitionSpec as P


R = 128
HALF = R // 2
QUARTER = HALF // 4
LEVELS = 8
F32 = jnp.float32
CORE_MASK = 1
TURNS = 4
RING_MASKS = (2, 4, 6)


def swap(value, mask):
    return lax.ppermute(value, "leaf", [(i, i ^ mask) for i in range(lax.axis_size("leaf"))])


def split(v):
    high = v.astype(jnp.bfloat16)
    return high, (v - high.astype(F32)).astype(jnp.bfloat16)


def dot_split(a, b, contract=(1, 0)):
    dims = (((contract[0],), (contract[1],)), ((), ()))

    def one(p, q):
        return lax.dot_general(p, q, dims, preferred_element_type=F32)

    return one(a[0], b[0]) + (one(a[0], b[1]) + one(a[1], b[0]))


def cols(parts, start, stop):
    return tuple(part[:, start:stop] for part in parts)


def row_blocks(first):
    offset = 0
    out = []
    for m in range(first, LEVELS):
        width = (LEVELS + 1 - m) * R
        out.append((m, offset, width))
        offset += width
    return out, offset


def spd_inverse(rows):
    shape = (8, R)
    sub = lax.broadcasted_iota(jnp.int32, shape, 0)
    lane = lax.broadcasted_iota(jnp.int32, shape, 1)

    def spread_row(v, i):
        return jnp.broadcast_to(v[i : i + 1, :], shape)

    def spread_col(v, k):
        return jnp.broadcast_to(v[:, k : k + 1], shape)

    count = R // 8
    turns = TURNS
    per_turn = count // turns

    def add_up(terms):
        while len(terms) > 1:
            terms = [a + b for a, b in zip(terms[::2], terms[1::2])]
        return terms[0]

    def eliminate(rows, p):
        base = 8 * p
        panel_rows = [spread_row(rows[p], j) for j in range(8)]
        d = [spread_col(rows[p], base + j) for j in range(8)]
        for a in range(0, 8, 2):
            b = a + 1
            ra = [spread_row(d[j], a) for j in range(8)]
            rb = [spread_row(d[j], b) for j in range(8)]
            inv_det = 1.0 / (ra[a] * rb[b] - ra[b] * rb[a])
            ma, mb = sub == a, sub == b
            va = jnp.where(ma, -rb[b], jnp.where(mb, rb[a], d[a] * rb[b] - d[b] * rb[a]))
            vb = jnp.where(ma, ra[b], jnp.where(mb, -ra[a], d[b] * ra[a] - d[a] * ra[b]))
            for j in range(8):
                if j == a:
                    d[j] = -(va * inv_det)
                elif j == b:
                    d[j] = -(vb * inv_det)
                else:
                    d[j] = jnp.where(ma | mb, 0.0, d[j]) - (va * ra[j] + vb * rb[j]) * inv_det
        inside = (lane >= base) & (lane < base + 8)
        panel = add_up(
            [d[j] * jnp.where(inside, jnp.where(lane == base + j, 1.0, 0.0), panel_rows[j]) for j in range(8)]
        )
        after = (p + 1) % count
        ahead = add_up([spread_col(rows[after], base + j) * spread_row(panel, j) for j in range(8)])
        ahead = jnp.where(inside, 0.0, rows[after]) - ahead
        zeros = [jnp.zeros((8, R), F32)]
        pivot_rows = jnp.concatenate(zeros * p + [panel] + zeros * (count - 1 - p), axis=0)
        change = dot_split(split(jnp.concatenate(rows, axis=0)), split(pivot_rows))
        result = [jnp.where(inside, 0.0, row) - change[8 * i : 8 * i + 8, :] for i, row in enumerate(rows)]
        result[p], result[after] = panel, ahead
        return result

    def turn(_, rows):
        rows = list(rows)
        for p in range(per_turn):
            rows = eliminate(rows, p)
        rows = rows[per_turn:] + rows[:per_turn]
        return tuple(pltpu.roll(row, R - 8 * per_turn, 1) for row in rows)

    return list(lax.fori_loop(0, turns, turn, tuple(rows)))


def vmem(n):
    return [pl.BlockSpec(memory_space=pltpu.VMEM)] * n


def smem():
    return [pl.BlockSpec(memory_space=pltpu.SMEM)]


def out(*shape):
    return jax.ShapeDtypeStruct(shape, F32)


def call(kernel, outs, args, index=None, scratch=(), flops=0):
    moved = 4 * (sum(a.size for a in args) + sum(o.size for o in outs))
    head = [] if index is None else [index]
    return pl.pallas_call(
        kernel,
        out_shape=outs,
        in_specs=(smem() if head else []) + vmem(len(args)),
        out_specs=vmem(len(outs)),
        scratch_shapes=list(scratch),
        cost_estimate=pl.CostEstimate(flops=flops, bytes_accessed=moved, transcendentals=0),
        compiler_params=pltpu.CompilerParams(vmem_limit_bytes=16 << 20),
    )(*head, *args)


CHUNK = 256


def chunk_span(r):
    return pl.ds(pl.multiple_of(r * CHUNK, CHUNK), CHUNK)


def stream(lo, hi, hbm, vmem_refs, sems, split_refs, use):
    (a_hbm, u_hbm, w_hbm), (a, u, w), (a_sem, sem) = hbm, vmem_refs, sems
    high, low = split_refs
    chunks = a.shape[0]
    copies = [
        pltpu.make_async_copy(u_hbm.at[:, lo:hi], u.at[:, lo:hi], sem.at[0]),
        pltpu.make_async_copy(u_hbm.at[:, hi:], u.at[:, hi:], sem.at[1]),
        pltpu.make_async_copy(w_hbm, w, sem.at[2]),
    ]

    def a_copy(r):
        return pltpu.make_async_copy(a_hbm.at[pl.ds(r * CHUNK, CHUNK), :], a.at[r], a_sem.at[r])

    copies[0].start()
    a_copy(0).start()
    copies[1].start()
    copies[2].start()
    for r in range(1, chunks):
        a_copy(r).start()
    copies[0].wait()
    high[...], low[...] = split(u[:, lo:hi])

    @pl.loop(0, chunks)
    def _(r):
        a_copy(r).wait()
        x = dot_split(split(a[r]), (high[...], low[...]))

        @pl.when(r == 0)
        def _():
            copies[1].wait()
            copies[2].wait()

        use(chunk_span(r), x)


def row0_kernel(a_hbm, u_hbm, w_hbm, x_ref, row_ref, a, u, w, high, low, a_sem, sem):
    row_ref[...] = jnp.zeros_like(row_ref)

    def use(span, x):
        x_ref[span, :] = x
        x = split(x)
        row_ref[:, : LEVELS * R] += dot_split(x, split(u[span, :]), (0, 0))
        row_ref[:, LEVELS * R :] += dot_split(x, split(w[span, :]), (0, 0))

    stream(0, R, (a_hbm, u_hbm, w_hbm), (a, u, w), (a_sem, sem), (high, low), use)


def rows12_kernel(
    index_ref, a_hbm, u_hbm, w_hbm, x_ref, pack_ref, keep_ref, total, a, u, w, high, low, a_sem, sem
):
    core = index_ref[0] & 1
    last = (LEVELS - 1) * R
    total[...] = jnp.zeros_like(total)

    def use(span, x):
        x_ref[span, :] = x
        x = split(x)
        total[:, :last] += dot_split(x, split(u[span, R:]), (0, 0))
        total[:, last:] += dot_split(x, split(w[span, :]), (0, 0))

    stream(R, 3 * R, (a_hbm, u_hbm, w_hbm), (a, u, w), (a_sem, sem), (high, low), use)
    pack_ref[:R, :] = total[:R, :]
    first, second = total[R : R + HALF, R:], total[R + HALF :, R:]
    keep_ref[...] = jnp.where(core == 0, first, second)
    pack_ref[R:, :last] = jnp.where(core == 0, second, first)
    pack_ref[R:, last:] = jnp.zeros((HALF, R), F32)


def stream_call(kernel, outs, args, width, grant, index=None, scratch=()):
    leaf = args[0].shape[0]
    head_args = () if index is None else (index,)
    return pl.pallas_call(
        kernel,
        out_shape=outs,
        in_specs=(smem() if head_args else []) + [pl.BlockSpec(memory_space=pltpu.HBM)] * 3,
        out_specs=vmem(len(outs)),
        scratch_shapes=[
            *scratch,
            pltpu.VMEM((leaf // CHUNK, CHUNK, leaf), F32),
            pltpu.VMEM((leaf, LEVELS * R), F32),
            pltpu.VMEM((leaf, R), F32),
            pltpu.VMEM((leaf, width), jnp.bfloat16),
            pltpu.VMEM((leaf, width), jnp.bfloat16),
            pltpu.SemaphoreType.DMA((leaf // CHUNK,)),
            pltpu.SemaphoreType.DMA((3,)),
        ],
        cost_estimate=pl.CostEstimate(
            flops=6 * leaf * 17 * R * width, bytes_accessed=8 * leaf * leaf, transcendentals=0
        ),
        compiler_params=pltpu.CompilerParams(vmem_limit_bytes=grant << 20),
    )(*head_args, *args)


def tail_solve_kernel(a_ref, u_ref, w_ref, x_ref, high_ref, low_ref):
    tail = (LEVELS - 3) * R
    high_ref[:, :tail], low_ref[:, :tail] = split(u_ref[:, 3 * R :])
    high_ref[:, tail:], low_ref[:, tail:] = split(w_ref[...])

    @pl.loop(0, 4)
    def _(r):
        rows = pl.ds(pl.multiple_of(r * 2 * R, 2 * R), 2 * R)
        x_ref[rows, :] = dot_split(split(a_ref[rows, :]), (high_ref[...], low_ref[...]))


def rest_rows_kernel(index_ref, u_ref, x_ref, keep_ref, send_ref, total):
    core = index_ref[0] & 1
    total[...] = jnp.zeros_like(total)

    @pl.loop(0, u_ref.shape[0] // CHUNK)
    def _(r):
        span = chunk_span(r)
        x = split(x_ref[span, :])
        for m, at, width in row_blocks(3)[0]:
            u = split(u_ref[span, m * R : (m + 1) * R])
            total[:, at : at + width] += dot_split(u, cols(x, (m - 3) * R, (LEVELS - 2) * R), (0, 0))

    keep_ref[...] = jnp.where(core == 0, total[:HALF, :], total[HALF:, :])
    send_ref[...] = jnp.where(core == 0, total[HALF:, :], total[:HALF, :])


def invert_store(panel_ref, w_ref):
    rows = [panel_ref[8 * i : 8 * i + 8, :R] for i in range(R // 8)]
    sub = lax.broadcasted_iota(jnp.int32, (8, R), 0)
    lane = lax.broadcasted_iota(jnp.int32, (8, R), 1)
    rows = [row + jnp.where(lane == sub + 8 * i, 1.0, 0.0) for i, row in enumerate(rows)]
    inverse = split(jnp.concatenate(spd_inverse(rows), axis=0))
    w_ref[...] = dot_split(inverse, split(panel_ref[:, R:]))


def invert_sum_kernel(own_ref, got_ref, panel_ref, w_ref):
    panel_ref[...] = own_ref[...] + got_ref[...]
    invert_store(panel_ref, w_ref)


def invert_half_kernel(index_ref, own_ref, got_ref, panel_ref, w_ref):
    core = index_ref[0] & 1
    own, got = own_ref[...], got_ref[...]
    panel_ref[:HALF, :] = jnp.where(core == 0, own, got)
    panel_ref[HALF:, :] = jnp.where(core == 0, got, own)
    invert_store(panel_ref, w_ref)


def invert_ring_kernel(index_ref, own_ref, got_ref, panel_ref, w_ref):
    core = index_ref[0] & 1
    x = (index_ref[0] >> 1) & 3
    for k in range(4):
        at = QUARTER * jnp.bitwise_xor(x, k)
        mine = pl.multiple_of(core * HALF + at, QUARTER)
        other = pl.multiple_of((1 - core) * HALF + at, QUARTER)
        panel_ref[pl.ds(mine, QUARTER), :] = own_ref[k]
        panel_ref[pl.ds(other, QUARTER), :] = got_ref[k]
    invert_store(panel_ref, w_ref)


def invert(level, own, got, index):
    n = (LEVELS + 1 - level) * R
    outs = (out(R, n), out(R, n - R))
    flops = 6 * R * R * n + 2 * R * R * R * 40
    if level == 0:
        return call(invert_sum_kernel, outs, (own, got), flops=flops)
    kernel = invert_ring_kernel if 3 <= level <= 5 else invert_half_kernel
    return call(kernel, outs, (own, got), index=index, flops=flops)


def row1_kernel(index_ref, own_ref, got_ref, keep_ref, panel_ref, w_ref, row_ref, half_ref, half2_ref):
    core = index_ref[0] & 1
    w = split(w_ref[...])
    row = own_ref[:R, :] + got_ref[:R, :] - dot_split(split(panel_ref[:, R : 2 * R]), w, (0, 0))
    row_ref[...] = row
    half_ref[...] = jnp.where(core == 0, row[:HALF], row[HALF:])
    change = dot_split(split(panel_ref[:, 2 * R : 3 * R]), cols(w, R, LEVELS * R), (0, 0))
    change = jnp.where(core == 0, change[:HALF], change[HALF:])
    half2_ref[...] = keep_ref[...] + got_ref[R:, : (LEVELS - 1) * R] - change


def ahead_kernel(index_ref, own_ref, got_ref, panel_ref, w_ref, half_ref):
    core = index_ref[0] & 1
    change = dot_split(split(panel_ref[:, R : 2 * R]), split(w_ref[...]), (0, 0))
    half_ref[...] = own_ref[...] + got_ref[...] - jnp.where(core == 0, change[:HALF], change[HALF:])


def downdate(core, level, panel_ref, w_ref, rows):
    w = split(w_ref[...])
    for m, offset, width in rows:
        left = split(panel_ref[:, (m - level) * R : (m - level + 1) * R])
        full = dot_split(left, cols(w, (m - level - 1) * R, (LEVELS - level) * R), (0, 0))
        yield m, offset, width, jnp.where(core == 0, full[:HALF], full[HALF:])


def rest0_kernel(index_ref, own_ref, got_ref, panel_ref, w_ref, rest_ref):
    core = index_ref[0] & 1
    for m, at, width, change in downdate(core, 0, panel_ref, w_ref, row_blocks(3)[0]):
        span = slice(at, at + width)
        rest_ref[:, span] = own_ref[:, span] + got_ref[:, span] - change


def whole_downdate(level, panel_ref, w_ref, rows, scr):
    w = split(w_ref[...])
    for m, at, width in rows:
        left = split(panel_ref[:, (m - level) * R : (m - level + 1) * R])
        scr[:, at : at + width] = dot_split(left, cols(w, (m - level - 1) * R, (LEVELS - level) * R), (0, 0))


def quarter_at(index_ref, k):
    x = (index_ref[0] >> 1) & 3
    return QUARTER * jnp.bitwise_xor(x, k)


def update1_kernel(index_ref, rest_ref, panel_ref, w_ref, q0, q1, q2, q3, scr):
    core = index_ref[0] & 1
    whole_downdate(1, panel_ref, w_ref, row_blocks(3)[0], scr)
    for k, q in enumerate((q0, q1, q2, q3)):
        at = quarter_at(index_ref, k)
        mine = pl.multiple_of(at, QUARTER)
        both = pl.multiple_of(core * HALF + at, QUARTER)
        q[...] = rest_ref[pl.ds(mine, QUARTER), :] - scr[pl.ds(both, QUARTER), :]


def update_quarter_kernel(level):
    skip = (LEVELS + 1 - level) * R if level > 2 else 0

    def kernel(index_ref, rest_ref, panel_ref, w_ref, out_ref, scr):
        core = index_ref[0] & 1
        whole_downdate(level, panel_ref, w_ref, row_blocks(level + 1)[0], scr)
        at = pl.multiple_of(core * HALF + quarter_at(index_ref, 0), QUARTER)
        out_ref[...] = rest_ref[:, skip:] - scr[pl.ds(at, QUARTER), :]

    return kernel


def store_next(level, m, at, value, row_ref, rest_ref):
    if m == level + 1:
        row_ref[...] = value
    else:
        at -= (LEVELS - level) * R
        rest_ref[:, at : at + value.shape[1]] = value


def update5_kernel(index_ref, own_ref, panel_ref, w_ref, row_ref, rest_ref, scr):
    core = index_ref[0] & 1
    for k in range(4):
        at = pl.multiple_of(quarter_at(index_ref, k), QUARTER)
        scr[pl.ds(at, QUARTER), :] = own_ref[k]
    skip = (LEVELS + 1 - 5) * R
    for m, at, width, change in downdate(core, 5, panel_ref, w_ref, row_blocks(6)[0]):
        store_next(5, m, at, scr[:, skip + at : skip + at + width] - change, row_ref, rest_ref)


def update6_kernel(index_ref, own_ref, got_ref, panel_ref, w_ref, row_ref):
    core = index_ref[0] & 1
    for _, _, _, change in downdate(core, 6, panel_ref, w_ref, row_blocks(7)[0]):
        row_ref[...] = own_ref[...] + got_ref[...] - change


def last_kernel(solved_ref, w_ref, solution_ref):
    first = dot_split(split(solved_ref[:, :R]), split(w_ref[...]))
    solution_ref[...] = solved_ref[:, R:] - first


def solve_step_kernel(solved_ref, w_ref, next_ref):
    w = split(w_ref[...])

    @pl.loop(0, solved_ref.shape[0] // CHUNK)
    def _(r):
        span = pl.ds(pl.multiple_of(r * CHUNK, CHUNK), CHUNK)
        next_ref[span, :] = solved_ref[span, R:] - dot_split(split(solved_ref[span, :R]), w)


def solve_step(solved, w):
    rows, n = solved.shape[0], solved.shape[1] - R
    (result,) = call(solve_step_kernel, (out(rows, n),), (solved, w), flops=6 * rows * R * n)
    return result


def solve_four_kernel(x0_ref, x12_ref, tail_ref, w0, w1, w2, w3, next_ref, high, low):
    for j, w in ((3, w3), (2, w2), (1, w1), (0, w0)):
        mid = (3 - j) * R
        t = w[:, mid:]
        if j < 3:
            below = slice((j + 1) * R, 4 * R)
            t = t - dot_split(split(w[:, :mid]), (high[below, :], low[below, :]))
        high[j * R : (j + 1) * R, :], low[j * R : (j + 1) * R, :] = split(t)

    @pl.loop(0, x0_ref.shape[0] // CHUNK)
    def _(r):
        span = pl.ds(pl.multiple_of(r * CHUNK, CHUNK), CHUNK)
        x = jnp.concatenate([x0_ref[span, :], x12_ref[span, :], tail_ref[span, :R]], axis=1)
        change = dot_split(split(x), (high[...], low[...]))
        next_ref[span, :] = tail_ref[span, R:] - change


def update_flops(level):
    return sum(6 * R * R * width for _, _, width in row_blocks(level + 1)[0])


def ring_all(value):
    return jnp.stack([value] + [swap(value, mask) for mask in RING_MASKS])


def tree_solve(white_noise, leaf_inverse, bases):
    index = lax.axis_index("leaf").astype(jnp.int32).reshape(1)
    leaf = leaf_inverse.shape[0]
    leaf_args = (leaf_inverse, bases, white_noise)
    x0, row0 = stream_call(row0_kernel, (out(leaf, R), out(R, 9 * R)), leaf_args, R, 56)
    got0 = swap(row0, CORE_MASK)
    x12, pack, keep2 = stream_call(
        rows12_kernel,
        (out(leaf, 2 * R), out(R + HALF, 8 * R), out(HALF, 7 * R)),
        leaf_args,
        2 * R,
        50,
        index=index,
        scratch=(pltpu.VMEM((2 * R, 8 * R), F32),),
    )
    got12 = swap(pack, CORE_MASK)
    weights = []
    panel, w = invert(0, row0, got0, index)
    weights.append(w)
    row1, half, half2 = call(
        row1_kernel,
        (out(R, 8 * R), out(HALF, 8 * R), out(HALF, 7 * R)),
        (pack, got12, keep2, panel, w),
        index=index,
        flops=90 * R**3,
    )
    got = swap(half, 2)
    (x_tail,) = call(
        tail_solve_kernel,
        (out(leaf, 6 * R),),
        (leaf_inverse, bases, white_noise),
        scratch=(pltpu.VMEM((leaf, 6 * R), jnp.bfloat16),) * 2,
        flops=6 * leaf * leaf * 6 * R,
    )
    width3 = row_blocks(3)[1]
    keep, send = call(
        rest_rows_kernel,
        (out(HALF, width3), out(HALF, width3)),
        (bases, x_tail),
        index=index,
        scratch=(pltpu.VMEM((R, width3), F32),),
        flops=6 * leaf * R * width3,
    )
    got_rest = swap(send, CORE_MASK)
    (rest,) = call(rest0_kernel, (out(HALF, width3),), (keep, got_rest, panel, w), index=index, flops=update_flops(2))
    half2_after, got = lax.optimization_barrier((half2, got))
    got2 = swap(half2_after, 2)
    half = half + got
    panel, w = invert(1, half, swap(half, CORE_MASK), index)
    weights.append(w)
    (half,) = call(ahead_kernel, (out(HALF, 7 * R),), (half2, got2, panel, w), index=index, flops=42 * R**3)
    got = swap(half, 4)
    quarters = call(
        update1_kernel,
        (out(QUARTER, width3),) * 4,
        (rest, row1, w),
        index=index,
        scratch=(pltpu.VMEM((R, width3), F32),),
        flops=update_flops(2),
    )
    half = half + got
    other = swap(half, CORE_MASK)
    panel, w = invert(2, half, other, index)
    weights.append(w)
    rest = quarters[0]
    for k in (1, 2, 0):
        part = swap(quarters[1 + k], RING_MASKS[k])
        rest = rest + part
    for level in range(2, 6):
        width = (LEVELS + 1 - level) * R
        if level > 2:
            got_rest = swap(rest, 1 << level)
            rest = rest + got_rest
            if level < 5:
                row = ring_all(rest[:, :width])
            else:
                rest = ring_all(rest)
                row = rest[:, :, :width]
            panel, w = invert(level, row, swap(row, CORE_MASK), index)
            weights.append(w)
        next_width = row_blocks(level + 1)[1]
        if level < 5:
            (rest,) = call(
                update_quarter_kernel(level),
                (out(QUARTER, next_width),),
                (rest, panel, w),
                index=index,
                scratch=(pltpu.VMEM((R, next_width), F32),),
                flops=update_flops(level),
            )
        else:
            half, rest = call(
                update5_kernel,
                (out(HALF, 3 * R), out(HALF, 2 * R)),
                (rest, panel, w),
                index=index,
                scratch=(pltpu.VMEM((HALF, 9 * R), F32),),
                flops=update_flops(level),
            )
        if level == 3:
            (solved,) = call(
                solve_four_kernel,
                (out(leaf, 5 * R),),
                (x0, x12, x_tail, *weights),
                scratch=(pltpu.VMEM((4 * R, 5 * R), jnp.bfloat16),) * 2,
                flops=6 * leaf * 4 * R * 5 * R,
            )
        elif level > 3:
            solved = solve_step(solved, w)
    got = swap(half, 64)
    got_rest = swap(rest, 64)
    half = half + got
    panel, w = invert(6, half, swap(half, CORE_MASK), index)
    solved = solve_step(solved, w)
    (half,) = call(update6_kernel, (out(HALF, 2 * R),), (rest, got_rest, panel, w), index=index, flops=update_flops(6))
    got = swap(half, 128)
    half = half + got
    _, w = invert(7, half, swap(half, CORE_MASK), index)
    (answer,) = call(last_kernel, (out(leaf, R),), (solved, w), flops=6 * leaf * R * R)
    return answer


def solution(mesh):
    in_specs = (P("leaf", None), P("leaf", None), P("leaf", None))
    out_specs = P("leaf", None)
    return jax.shard_map(tree_solve, mesh=mesh, in_specs=in_specs, out_specs=out_specs, check_vma=False)
```

```python
import jax
import jax.numpy as jnp
from jax import lax
from jax.experimental import pallas as pl
from jax.experimental.pallas import tpu as pltpu
from jax.sharding import PartitionSpec as P


R = 128
HALF = R // 2
QUARTER = HALF // 4
LEVELS = 8
F32 = jnp.float32
CORE_MASK = 1
TURNS = 4
RING_MASKS = (2, 4, 6)


def swap(value, mask):
    return lax.ppermute(value, "leaf", [(i, i ^ mask) for i in range(lax.axis_size("leaf"))])


def split(v):
    high = v.astype(jnp.bfloat16)
    return high, (v - high.astype(F32)).astype(jnp.bfloat16)


def dot_split(a, b, contract=(1, 0)):
    dims = (((contract[0],), (contract[1],)), ((), ()))

    def one(p, q):
        return lax.dot_general(p, q, dims, preferred_element_type=F32)

    return one(a[0], b[0]) + (one(a[0], b[1]) + one(a[1], b[0]))


def cols(parts, start, stop):
    return tuple(part[:, start:stop] for part in parts)


def row_blocks(first):
    offset = 0
    out = []
    for m in range(first, LEVELS):
        width = (LEVELS + 1 - m) * R
        out.append((m, offset, width))
        offset += width
    return out, offset


def spd_inverse(rows):
    shape = (8, R)
    sub = lax.broadcasted_iota(jnp.int32, shape, 0)
    lane = lax.broadcasted_iota(jnp.int32, shape, 1)

    def spread_row(v, i):
        return jnp.broadcast_to(v[i : i + 1, :], shape)

    def spread_col(v, k):
        return jnp.broadcast_to(v[:, k : k + 1], shape)

    count = R // 8
    turns = TURNS
    per_turn = count // turns

    def add_up(terms):
        while len(terms) > 1:
            terms = [a + b for a, b in zip(terms[::2], terms[1::2])]
        return terms[0]

    def eliminate(rows, p):
        base = 8 * p
        panel_rows = [spread_row(rows[p], j) for j in range(8)]
        d = [spread_col(rows[p], base + j) for j in range(8)]
        for a in range(0, 8, 2):
            b = a + 1
            ra = [spread_row(d[j], a) for j in range(8)]
            rb = [spread_row(d[j], b) for j in range(8)]
            inv_det = 1.0 / (ra[a] * rb[b] - ra[b] * rb[a])
            ma, mb = sub == a, sub == b
            va = jnp.where(ma, -rb[b], jnp.where(mb, rb[a], d[a] * rb[b] - d[b] * rb[a]))
            vb = jnp.where(ma, ra[b], jnp.where(mb, -ra[a], d[b] * ra[a] - d[a] * ra[b]))
            for j in range(8):
                if j == a:
                    d[j] = -(va * inv_det)
                elif j == b:
                    d[j] = -(vb * inv_det)
                else:
                    d[j] = jnp.where(ma | mb, 0.0, d[j]) - (va * ra[j] + vb * rb[j]) * inv_det
        inside = (lane >= base) & (lane < base + 8)
        panel = add_up(
            [d[j] * jnp.where(inside, jnp.where(lane == base + j, 1.0, 0.0), panel_rows[j]) for j in range(8)]
        )
        after = (p + 1) % count
        ahead = add_up([spread_col(rows[after], base + j) * spread_row(panel, j) for j in range(8)])
        ahead = jnp.where(inside, 0.0, rows[after]) - ahead
        zeros = [jnp.zeros((8, R), F32)]
        pivot_rows = jnp.concatenate(zeros * p + [panel] + zeros * (count - 1 - p), axis=0)
        change = dot_split(split(jnp.concatenate(rows, axis=0)), split(pivot_rows))
        result = [jnp.where(inside, 0.0, row) - change[8 * i : 8 * i + 8, :] for i, row in enumerate(rows)]
        result[p], result[after] = panel, ahead
        return result

    def turn(_, rows):
        rows = list(rows)
        for p in range(per_turn):
            rows = eliminate(rows, p)
        rows = rows[per_turn:] + rows[:per_turn]
        return tuple(pltpu.roll(row, R - 8 * per_turn, 1) for row in rows)

    return list(lax.fori_loop(0, turns, turn, tuple(rows)))


def vmem(n):
    return [pl.BlockSpec(memory_space=pltpu.VMEM)] * n


def smem():
    return [pl.BlockSpec(memory_space=pltpu.SMEM)]


def out(*shape):
    return jax.ShapeDtypeStruct(shape, F32)


def call(kernel, outs, args, index=None, scratch=(), flops=0):
    moved = 4 * (sum(a.size for a in args) + sum(o.size for o in outs))
    head = [] if index is None else [index]
    return pl.pallas_call(
        kernel,
        out_shape=outs,
        in_specs=(smem() if head else []) + vmem(len(args)),
        out_specs=vmem(len(outs)),
        scratch_shapes=list(scratch),
        cost_estimate=pl.CostEstimate(flops=flops, bytes_accessed=moved, transcendentals=0),
        compiler_params=pltpu.CompilerParams(vmem_limit_bytes=16 << 20),
    )(*head, *args)


HEAD = 3 * R
CHUNK = 256


def head_kernel(
    index_ref, a_hbm, u_hbm, w_hbm, x_ref, rows_ref, keep_ref, send_ref, a, u, w, u_high, u_low, row2, a_sem, sem
):
    core = index_ref[0] & 1
    chunks = a.shape[0]
    copies = [
        pltpu.make_async_copy(u_hbm.at[:, :HEAD], u.at[:, :HEAD], sem.at[0]),
        pltpu.make_async_copy(u_hbm.at[:, HEAD:], u.at[:, HEAD:], sem.at[1]),
        pltpu.make_async_copy(w_hbm, w, sem.at[2]),
    ]

    def a_copy(r):
        return pltpu.make_async_copy(a_hbm.at[pl.ds(r * CHUNK, CHUNK), :], a.at[r], a_sem.at[r])

    copies[0].start()
    a_copy(0).start()
    copies[1].start()
    copies[2].start()
    for r in range(1, chunks):
        a_copy(r).start()
    copies[0].wait()
    u_high[...], u_low[...] = split(u[:, :HEAD])
    rows_ref[...] = jnp.zeros_like(rows_ref)
    row2[...] = jnp.zeros_like(row2)

    @pl.loop(0, chunks)
    def _(r):
        a_copy(r).wait()
        span = pl.ds(pl.multiple_of(r * CHUNK, CHUNK), CHUNK)
        x = dot_split(split(a[r]), (u_high[...], u_low[...]))
        x_ref[span, :] = x

        @pl.when(r == 0)
        def _():
            copies[1].wait()
            copies[2].wait()

        x = split(x)
        chunk_u, chunk_w = split(u[span, :]), split(w[span, :])
        at = 0
        for m in range(3):
            left = cols(x, m * R, (m + 1) * R)
            width = (LEVELS - m) * R
            piece = dot_split(left, cols(chunk_u, m * R, LEVELS * R), (0, 0))
            noise = dot_split(left, chunk_w, (0, 0))
            if m < 2:
                rows_ref[:, at : at + width] += piece
                rows_ref[:, at + width : at + width + R] += noise
                at += width + R
            else:
                row2[:, :width] += piece
                row2[:, width:] += noise

    keep_ref[...] = jnp.where(core == 0, row2[:HALF, :], row2[HALF:, :])
    send_ref[...] = jnp.where(core == 0, row2[HALF:, :], row2[:HALF, :])


def head(index, leaf_inverse, bases, white_noise):
    leaf = leaf_inverse.shape[0]
    n2 = (LEVELS - 1) * R
    return pl.pallas_call(
        head_kernel,
        name="head",
        out_shape=(out(leaf, HEAD), out(R, 17 * R), out(HALF, n2), out(HALF, n2)),
        in_specs=smem() + [pl.BlockSpec(memory_space=pltpu.HBM)] * 3,
        out_specs=vmem(4),
        scratch_shapes=[
            pltpu.VMEM((leaf // CHUNK, CHUNK, leaf), F32),
            pltpu.VMEM((leaf, LEVELS * R), F32),
            pltpu.VMEM((leaf, R), F32),
            pltpu.VMEM((leaf, HEAD), jnp.bfloat16),
            pltpu.VMEM((leaf, HEAD), jnp.bfloat16),
            pltpu.VMEM((R, n2), F32),
            pltpu.SemaphoreType.DMA((leaf // CHUNK,)),
            pltpu.SemaphoreType.DMA((3,)),
        ],
        cost_estimate=pl.CostEstimate(flops=6 * leaf * R * 54 * R, bytes_accessed=8 * leaf * leaf, transcendentals=0),
        compiler_params=pltpu.CompilerParams(vmem_limit_bytes=56 << 20),
    )(index, leaf_inverse, bases, white_noise)


def tail_solve_kernel(a_ref, u_ref, w_ref, x_ref, high_ref, low_ref):
    tail = (LEVELS - 3) * R
    high_ref[:, :tail], low_ref[:, :tail] = split(u_ref[:, 3 * R :])
    high_ref[:, tail:], low_ref[:, tail:] = split(w_ref[...])

    @pl.loop(0, 4)
    def _(r):
        rows = pl.ds(pl.multiple_of(r * 2 * R, 2 * R), 2 * R)
        x_ref[rows, :] = dot_split(split(a_ref[rows, :]), (high_ref[...], low_ref[...]))


def rest_rows_kernel(index_ref, u_ref, x_ref, keep_ref, send_ref):
    core = index_ref[0] & 1
    x = split(x_ref[...])
    for m, at, width in row_blocks(3)[0]:
        u = split(u_ref[:, m * R : (m + 1) * R])
        piece = dot_split(u, cols(x, (m - 3) * R, (LEVELS - 2) * R), (0, 0))
        keep_ref[:, at : at + width] = jnp.where(core == 0, piece[:HALF], piece[HALF:])
        send_ref[:, at : at + width] = jnp.where(core == 0, piece[HALF:], piece[:HALF])


def invert_store(panel_ref, w_ref):
    rows = [panel_ref[8 * i : 8 * i + 8, :R] for i in range(R // 8)]
    sub = lax.broadcasted_iota(jnp.int32, (8, R), 0)
    lane = lax.broadcasted_iota(jnp.int32, (8, R), 1)
    rows = [row + jnp.where(lane == sub + 8 * i, 1.0, 0.0) for i, row in enumerate(rows)]
    inverse = split(jnp.concatenate(spd_inverse(rows), axis=0))
    w_ref[...] = dot_split(inverse, split(panel_ref[:, R:]))


def invert_sum_kernel(own_ref, got_ref, panel_ref, w_ref):
    n = panel_ref.shape[1]
    panel_ref[...] = own_ref[:, :n] + got_ref[:, :n]
    invert_store(panel_ref, w_ref)


def invert_half_kernel(index_ref, own_ref, got_ref, panel_ref, w_ref):
    core = index_ref[0] & 1
    own, got = own_ref[...], got_ref[...]
    panel_ref[:HALF, :] = jnp.where(core == 0, own, got)
    panel_ref[HALF:, :] = jnp.where(core == 0, got, own)
    invert_store(panel_ref, w_ref)


def invert_ring_kernel(index_ref, own_ref, got_ref, panel_ref, w_ref):
    core = index_ref[0] & 1
    x = (index_ref[0] >> 1) & 3
    for k in range(4):
        at = QUARTER * jnp.bitwise_xor(x, k)
        mine = pl.multiple_of(core * HALF + at, QUARTER)
        other = pl.multiple_of((1 - core) * HALF + at, QUARTER)
        panel_ref[pl.ds(mine, QUARTER), :] = own_ref[k]
        panel_ref[pl.ds(other, QUARTER), :] = got_ref[k]
    invert_store(panel_ref, w_ref)


def invert(level, own, got, index):
    n = (LEVELS + 1 - level) * R
    outs = (out(R, n), out(R, n - R))
    flops = 6 * R * R * n + 2 * R * R * R * 40
    if level == 0:
        return call(invert_sum_kernel, outs, (own, got), flops=flops)
    kernel = invert_ring_kernel if 3 <= level <= 5 else invert_half_kernel
    return call(kernel, outs, (own, got), index=index, flops=flops)


def stage_kernel(rows_ref, staged_ref):
    staged_ref[...] = rows_ref[...]


def row1_kernel(index_ref, own_ref, got_ref, keep_ref, got2_ref, panel_ref, w_ref, row_ref, half_ref, half2_ref):
    core = index_ref[0] & 1
    w = split(w_ref[...])
    row = own_ref[:, 9 * R :] + got_ref[:, 9 * R :] - dot_split(split(panel_ref[:, R : 2 * R]), w, (0, 0))
    row_ref[...] = row
    half_ref[...] = jnp.where(core == 0, row[:HALF], row[HALF:])
    change = dot_split(split(panel_ref[:, 2 * R : 3 * R]), cols(w, R, LEVELS * R), (0, 0))
    half2_ref[...] = keep_ref[...] + got2_ref[...] - jnp.where(core == 0, change[:HALF], change[HALF:])


def ahead_kernel(index_ref, own_ref, got_ref, panel_ref, w_ref, half_ref):
    core = index_ref[0] & 1
    change = dot_split(split(panel_ref[:, R : 2 * R]), split(w_ref[...]), (0, 0))
    half_ref[...] = own_ref[...] + got_ref[...] - jnp.where(core == 0, change[:HALF], change[HALF:])


def downdate(core, level, panel_ref, w_ref, rows):
    w = split(w_ref[...])
    for m, offset, width in rows:
        left = split(panel_ref[:, (m - level) * R : (m - level + 1) * R])
        full = dot_split(left, cols(w, (m - level - 1) * R, (LEVELS - level) * R), (0, 0))
        yield m, offset, width, jnp.where(core == 0, full[:HALF], full[HALF:])


def rest0_kernel(index_ref, own_ref, got_ref, panel_ref, w_ref, rest_ref):
    core = index_ref[0] & 1
    for m, at, width, change in downdate(core, 0, panel_ref, w_ref, row_blocks(3)[0]):
        span = slice(at, at + width)
        rest_ref[:, span] = own_ref[:, span] + got_ref[:, span] - change


def whole_downdate(level, panel_ref, w_ref, rows, scr):
    w = split(w_ref[...])
    for m, at, width in rows:
        left = split(panel_ref[:, (m - level) * R : (m - level + 1) * R])
        scr[:, at : at + width] = dot_split(left, cols(w, (m - level - 1) * R, (LEVELS - level) * R), (0, 0))


def quarter_at(index_ref, k):
    x = (index_ref[0] >> 1) & 3
    return QUARTER * jnp.bitwise_xor(x, k)


def update1_kernel(index_ref, rest_ref, panel_ref, w_ref, q0, q1, q2, q3, scr):
    core = index_ref[0] & 1
    whole_downdate(1, panel_ref, w_ref, row_blocks(3)[0], scr)
    for k, q in enumerate((q0, q1, q2, q3)):
        at = quarter_at(index_ref, k)
        mine = pl.multiple_of(at, QUARTER)
        both = pl.multiple_of(core * HALF + at, QUARTER)
        q[...] = rest_ref[pl.ds(mine, QUARTER), :] - scr[pl.ds(both, QUARTER), :]


def update_quarter_kernel(level):
    skip = (LEVELS + 1 - level) * R if level > 2 else 0

    def kernel(index_ref, rest_ref, panel_ref, w_ref, out_ref, scr):
        core = index_ref[0] & 1
        whole_downdate(level, panel_ref, w_ref, row_blocks(level + 1)[0], scr)
        at = pl.multiple_of(core * HALF + quarter_at(index_ref, 0), QUARTER)
        out_ref[...] = rest_ref[:, skip:] - scr[pl.ds(at, QUARTER), :]

    return kernel


def store_next(level, m, at, value, row_ref, rest_ref):
    if m == level + 1:
        row_ref[...] = value
    else:
        at -= (LEVELS - level) * R
        rest_ref[:, at : at + value.shape[1]] = value


def update5_kernel(index_ref, own_ref, panel_ref, w_ref, row_ref, rest_ref, scr):
    core = index_ref[0] & 1
    for k in range(4):
        at = pl.multiple_of(quarter_at(index_ref, k), QUARTER)
        scr[pl.ds(at, QUARTER), :] = own_ref[k]
    skip = (LEVELS + 1 - 5) * R
    for m, at, width, change in downdate(core, 5, panel_ref, w_ref, row_blocks(6)[0]):
        store_next(5, m, at, scr[:, skip + at : skip + at + width] - change, row_ref, rest_ref)


def update6_kernel(index_ref, own_ref, got_ref, panel_ref, w_ref, row_ref):
    core = index_ref[0] & 1
    for _, _, _, change in downdate(core, 6, panel_ref, w_ref, row_blocks(7)[0]):
        row_ref[...] = own_ref[...] + got_ref[...] - change


def last_kernel(solved_ref, w_ref, solution_ref):
    first = dot_split(split(solved_ref[:, :R]), split(w_ref[...]))
    solution_ref[...] = solved_ref[:, R:] - first


def solve_step_kernel(solved_ref, w_ref, next_ref):
    w = split(w_ref[...])

    @pl.loop(0, solved_ref.shape[0] // CHUNK)
    def _(r):
        span = pl.ds(pl.multiple_of(r * CHUNK, CHUNK), CHUNK)
        next_ref[span, :] = solved_ref[span, R:] - dot_split(split(solved_ref[span, :R]), w)


def solve_step(solved, w):
    rows, n = solved.shape[0], solved.shape[1] - R
    (result,) = call(solve_step_kernel, (out(rows, n),), (solved, w), flops=6 * rows * R * n)
    return result


def solve_four_kernel(head_ref, tail_ref, w0, w1, w2, w3, next_ref, high, low):
    for j, w in ((3, w3), (2, w2), (1, w1), (0, w0)):
        mid = (3 - j) * R
        t = w[:, mid:]
        if j < 3:
            below = slice((j + 1) * R, 4 * R)
            t = t - dot_split(split(w[:, :mid]), (high[below, :], low[below, :]))
        high[j * R : (j + 1) * R, :], low[j * R : (j + 1) * R, :] = split(t)

    @pl.loop(0, head_ref.shape[0] // CHUNK)
    def _(r):
        span = pl.ds(pl.multiple_of(r * CHUNK, CHUNK), CHUNK)
        change = dot_split(split(head_ref[span, :]), (high[:HEAD, :], low[:HEAD, :]))
        change = change + dot_split(split(tail_ref[span, :R]), (high[HEAD:, :], low[HEAD:, :]))
        next_ref[span, :] = tail_ref[span, R:] - change


def update_flops(level):
    return sum(6 * R * R * width for _, _, width in row_blocks(level + 1)[0])


def ring_all(value):
    return jnp.stack([value] + [swap(value, mask) for mask in RING_MASKS])


def tree_solve(white_noise, leaf_inverse, bases):
    index = lax.axis_index("leaf").astype(jnp.int32).reshape(1)
    leaf = leaf_inverse.shape[0]
    x_head, rows01, keep2, send2 = head(index, leaf_inverse, bases, white_noise)
    got01 = swap(rows01, CORE_MASK)
    (rows01,) = call(stage_kernel, (out(R, 17 * R),), (rows01,))
    got2 = swap(send2, CORE_MASK)
    weights = []
    panel, w = invert(0, rows01, got01, index)
    weights.append(w)
    row1, half, half2 = call(
        row1_kernel,
        (out(R, 8 * R), out(HALF, 8 * R), out(HALF, 7 * R)),
        (rows01, got01, keep2, got2, panel, w),
        index=index,
        flops=90 * R**3,
    )
    got = swap(half, 2)
    (x_tail,) = call(
        tail_solve_kernel,
        (out(leaf, 6 * R),),
        (leaf_inverse, bases, white_noise),
        scratch=(pltpu.VMEM((leaf, 6 * R), jnp.bfloat16),) * 2,
        flops=6 * leaf * leaf * 6 * R,
    )
    width3 = row_blocks(3)[1]
    keep, send = call(
        rest_rows_kernel,
        (out(HALF, width3), out(HALF, width3)),
        (bases, x_tail),
        index=index,
        flops=6 * leaf * R * width3,
    )
    got_rest = swap(send, CORE_MASK)
    (rest,) = call(rest0_kernel, (out(HALF, width3),), (keep, got_rest, panel, w), index=index, flops=update_flops(2))
    half2_after, got = lax.optimization_barrier((half2, got))
    got2 = swap(half2_after, 2)
    half = half + got
    panel, w = invert(1, half, swap(half, CORE_MASK), index)
    weights.append(w)
    (half,) = call(ahead_kernel, (out(HALF, 7 * R),), (half2, got2, panel, w), index=index, flops=42 * R**3)
    got = swap(half, 4)
    quarters = call(
        update1_kernel,
        (out(QUARTER, width3),) * 4,
        (rest, row1, w),
        index=index,
        scratch=(pltpu.VMEM((R, width3), F32),),
        flops=update_flops(2),
    )
    half = half + got
    other = swap(half, CORE_MASK)
    panel, w = invert(2, half, other, index)
    weights.append(w)
    rest = quarters[0]
    for k in (1, 2, 0):
        part = swap(quarters[1 + k], RING_MASKS[k])
        rest = rest + part
    for level in range(2, 6):
        width = (LEVELS + 1 - level) * R
        if level > 2:
            got_rest = swap(rest, 1 << level)
            rest = rest + got_rest
            if level < 5:
                row = ring_all(rest[:, :width])
            else:
                rest = ring_all(rest)
                row = rest[:, :, :width]
            panel, w = invert(level, row, swap(row, CORE_MASK), index)
            weights.append(w)
        next_width = row_blocks(level + 1)[1]
        if level < 5:
            (rest,) = call(
                update_quarter_kernel(level),
                (out(QUARTER, next_width),),
                (rest, panel, w),
                index=index,
                scratch=(pltpu.VMEM((R, next_width), F32),),
                flops=update_flops(level),
            )
        else:
            half, rest = call(
                update5_kernel,
                (out(HALF, 3 * R), out(HALF, 2 * R)),
                (rest, panel, w),
                index=index,
                scratch=(pltpu.VMEM((HALF, 9 * R), F32),),
                flops=update_flops(level),
            )
        if level == 3:
            (solved,) = call(
                solve_four_kernel,
                (out(leaf, 5 * R),),
                (x_head, x_tail, *weights),
                scratch=(pltpu.VMEM((4 * R, 5 * R), jnp.bfloat16),) * 2,
                flops=6 * leaf * 4 * R * 5 * R,
            )
        elif level > 3:
            solved = solve_step(solved, w)
    got = swap(half, 64)
    got_rest = swap(rest, 64)
    half = half + got
    panel, w = invert(6, half, swap(half, CORE_MASK), index)
    solved = solve_step(solved, w)
    (half,) = call(update6_kernel, (out(HALF, 2 * R),), (rest, got_rest, panel, w), index=index, flops=update_flops(6))
    got = swap(half, 128)
    half = half + got
    _, w = invert(7, half, swap(half, CORE_MASK), index)
    (answer,) = call(last_kernel, (out(leaf, R),), (solved, w), flops=6 * leaf * R * R)
    return answer


def solution(mesh):
    in_specs = (P("leaf", None), P("leaf", None), P("leaf", None))
    out_specs = P("leaf", None)
    return jax.shard_map(tree_solve, mesh=mesh, in_specs=in_specs, out_specs=out_specs, check_vma=False)
```
